32 devices in a mesh: seq: 8 (over z, y), tp: 4 (over x, core).
Axes of the slice: x: 2, y: 2, z: 4, core: 2. Of those that a mesh axis runs over, the one named last changes fastest.
Arguments:
- glob_out: bfloat16 [3072, 8192], P('seq', 'tp'), may hold values from -6 to 6
- byte_ids: int32 [3072, 8], P(('seq', 'tp')), may hold values from 0 to 255
- out_grad: bfloat16 [24576, 1024], P(('seq', 'tp')), may hold values from -6 to 6
- embed: bfloat16 [256, 1024], replicated, may hold values from -6 to 6
- w_proj: bfloat16 [1024, 1024], replicated, may hold values from -0.1875 to 0.1875
- norm_gain: float32 [1024], replicated, may hold values from 0.5 to 1.5
- w_qkv: bfloat16 [1024, 3072], replicated, may hold values from -0.40625 to 0.40625
- w_out: bfloat16 [1024, 1024], replicated, may hold values from -0.1875 to 0.1875
Outputs:
- glob_grad: bfloat16 [3072, 8192], P('seq', 'tp')
- grad_embed: float32 [256, 1024], P(('seq', 'tp'))
- grad_proj: float32 [1024, 1024], P(('seq', 'tp'))
- grad_gain: float32 [1024], P(('seq', 'tp'))
- grad_qkv: float32 [1024, 3072], P(('seq', 'tp'))
- grad_out: float32 [1024, 1024], P(('seq', 'tp'))
The draws below stay inside these ranges and needn't reach their ends.
All inputs are finite; a program needn't handle non-finite values.
Results may differ from the reference program's by a relative error of at most 0.0075.
The reference program's roundings to bfloat16 on the way count: a program that leaves them out, or rounds other values in their place, can miss the bound.
Values may be sent and summed in bfloat16 or wider, within the bound.
No kernel may reach another device: no remote copies, remote signals or barrier semaphores. Data moves between devices by JAX's collectives and lax.ppermute only.
A program may use at most 192 MiB of HBM per device.

```python
import jax
import jax.numpy as jnp
from jax import lax

D = 1024
HEADS = 16
HEAD = 64
PATCH = 8
VOCAB = 256
GW = 8192
NPATCH = 3072
TOKENS = 24576


def draw_w_qkv(key, part):
    key_base = jax.random.fold_in(key, 0)
    matrix = jax.random.truncated_normal(key_base, -6.0, 6.0, (D, 3 * D), jnp.float32) * D ** (-0.5)
    return matrix.astype(jnp.bfloat16)


def place_ends(result, own_key, low, top_value):
    index_at = [jax.random.randint(jax.random.fold_in(own_key, axis), (), 0, length) for axis, length in enumerate(result.shape)]
    main_axis = result.shape.index(max(result.shape))
    next_to = index_at[:main_axis] + [(index_at[main_axis] + 1) % result.shape[main_axis]] + index_at[main_axis + 1:]
    return result.at[tuple(index_at)].set(low).at[tuple(next_to)].set(top_value)


def block_scale(key, dims, shards, least, top_value):
    loudness = 1.0
    for dim, shards_of in shards:
        heights = jax.random.uniform(jax.random.fold_in(jax.random.fold_in(key, 6), dim), (shards_of,), jnp.float32, least / len(shards), top_value / len(shards))
        loudness = loudness * jnp.repeat(jnp.exp(heights), dims[dim] // shards_of).reshape((-1,) + (1,) * (len(dims) - 1 - dim))
    return loudness


def centred(own_key, shape, spread, limit, cuts=(), kind=jnp.bfloat16):
    values = spread * jax.random.normal(own_key, shape, jnp.float32)
    if cuts:
        values = values * block_scale(own_key, shape, cuts, -0.22, 0.18)
    return jnp.clip(values, -limit, limit).astype(kind)


def setup_inputs(seed: int = 0) -> dict:
    seeds = jax.random.split(jax.random.key(seed), 9)
    glob_out = centred(seeds[0], (NPATCH, GW), 1.0, 6.0, ((0, 8), (1, 4)))
    byte_ids = place_ends(jax.random.randint(seeds[1], (NPATCH, PATCH), 0, VOCAB), jax.random.fold_in(seeds[1], 1), 0, VOCAB - 1).astype(jnp.int32)
    out_grad = centred(seeds[2], (TOKENS, D), 1.0, 6.0, ((0, 32),))
    embed = centred(seeds[3], (VOCAB, D), 1.0, 6.0)
    w_proj = centred(seeds[4], (D, D), D ** -0.5, 0.1875)
    norm_gain = jnp.clip(1.0 + 0.1 * jax.random.normal(seeds[5], (D,), jnp.float32), 0.5, 1.5)
    w_qkv = draw_w_qkv(jax.random.fold_in(seeds[8], 71), 0)
    w_out = centred(seeds[7], (D, D), D ** -0.5, 0.1875)
    return dict(glob_out=glob_out, byte_ids=byte_ids, out_grad=out_grad, embed=embed, w_proj=w_proj, norm_gain=norm_gain, w_qkv=w_qkv, w_out=w_out)


def reference(glob_out, byte_ids, out_grad, embed, w_proj, norm_gain, w_qkv, w_out):
    vocab, width = embed.shape
    scale = HEAD ** (-0.5)
    slices = glob_out.reshape(-1, width)
    ids = byte_ids.reshape(-1)
    onehot = (ids[:, None] == jnp.arange(vocab, dtype=jnp.int32)[None, :]).astype(jnp.bfloat16)
    x = jnp.dot(onehot, embed, preferred_element_type=jnp.float32) + jnp.dot(slices, w_proj, preferred_element_type=jnp.float32)
    inv = lax.rsqrt(lax.optimization_barrier(jnp.mean(x * x, axis=1, keepdims=True)) + 1e-05)
    normed = x * inv
    act = (normed * norm_gain).astype(jnp.bfloat16)
    qkv = jnp.dot(act, w_qkv, preferred_element_type=jnp.float32).astype(jnp.bfloat16)
    count = qkv.shape[0] // PATCH
    parts = qkv.reshape(count, PATCH, 3, HEADS, HEAD).astype(jnp.float32)
    query = parts[:, :, 0]
    keys = parts[:, :, 1]
    values = parts[:, :, 2]
    causal = jnp.arange(PATCH)[:, None] >= jnp.arange(PATCH)[None, :]
    scores = jnp.einsum('pihd,pjhd->phij', query, keys) * scale
    scores = jnp.where(causal, scores, -1e+30)
    peak = lax.optimization_barrier(jnp.max(scores, axis=-1, keepdims=True))
    expo = jnp.exp(scores - peak)
    probs = expo / lax.optimization_barrier(jnp.sum(expo, axis=-1, keepdims=True))
    probs_b = probs.astype(jnp.bfloat16).astype(jnp.float32)
    context = jnp.einsum('phij,pjhd->pihd', probs_b, values).reshape(-1, width).astype(jnp.bfloat16)
    grad_out = jnp.dot(context.T, out_grad, preferred_element_type=jnp.float32)
    d_context = jnp.dot(out_grad, w_out.T, preferred_element_type=jnp.float32).astype(jnp.bfloat16)
    d_context = d_context.reshape(count, PATCH, HEADS, HEAD).astype(jnp.float32)
    d_probs = jnp.einsum('pihd,pjhd->phij', d_context, values)
    d_scores = probs * (d_probs - lax.optimization_barrier(jnp.sum(probs * d_probs, axis=-1, keepdims=True))) * scale
    d_scores = jnp.where(causal, d_scores, 0.0).astype(jnp.bfloat16).astype(jnp.float32)
    d_query = jnp.einsum('phij,pjhd->pihd', d_scores, keys)
    d_key = jnp.einsum('phij,pihd->pjhd', d_scores, query)
    d_value = jnp.einsum('phij,pihd->pjhd', probs_b, d_context)
    d_qkv = jnp.stack([d_query, d_key, d_value], axis=2).reshape(-1, 3 * width).astype(jnp.bfloat16)
    grad_qkv = jnp.dot(act.T, d_qkv, preferred_element_type=jnp.float32)
    d_act = jnp.dot(d_qkv, w_qkv.T, preferred_element_type=jnp.float32)
    grad_gain = lax.optimization_barrier(jnp.sum(d_act * normed, axis=0))
    d_normed = d_act * norm_gain
    d_x = out_grad.astype(jnp.float32) + inv * (d_normed - normed * lax.optimization_barrier(jnp.mean(d_normed * normed, axis=1, keepdims=True)))
    d_x = d_x.astype(jnp.bfloat16)
    grad_embed = jnp.dot(onehot.T, d_x, preferred_element_type=jnp.float32)
    grad_proj = jnp.dot(slices.T, d_x, preferred_element_type=jnp.float32)
    glob_grad = jnp.dot(d_x, w_proj.T, preferred_element_type=jnp.float32).astype(jnp.bfloat16).reshape(glob_out.shape)
    return (glob_grad, grad_embed, grad_proj, grad_gain, grad_qkv, grad_out)
```

```python
import functools

import jax
import jax.numpy as jnp
from jax import lax
from jax.sharding import PartitionSpec as P

HEADS = 16
HEAD = 64
PATCH = 8


def bit_masks(mesh):
    seq, tp = mesh.shape["seq"], mesh.shape["tp"]
    tp_bits = [1 << b for b in range(tp.bit_length() - 1)]
    seq_bits = [tp << b for b in range(seq.bit_length() - 1)]
    return tp_bits, seq_bits


def spans(bits):
    masks = [0]
    for bit in bits:
        masks = masks + [m ^ bit for m in masks]
    return masks


def scatter_order(stages):
    order = [0]
    for bits in reversed(stages):
        order = [m ^ q for m in spans(bits) for q in order]
    return order


def exchange(block, mask, devices):
    return lax.ppermute(block, ("seq", "tp"), [(d, d ^ mask) for d in range(devices)])


def reduce_scatter(partial, stages, me, devices, wire=jnp.bfloat16):
    rows, cols = partial.shape
    order = jnp.array(scatter_order(stages), dtype=jnp.int32) ^ me
    blocks = partial.astype(wire).reshape(devices, rows // devices, cols)[order]
    for n, bits in enumerate(stages):
        masks = spans(bits)
        size = blocks.shape[0] // len(masks)
        total = blocks[:size].astype(jnp.float32)
        for k, mask in enumerate(masks):
            if k:
                got = exchange(blocks[k * size : (k + 1) * size], mask, devices)
                total = total + got.astype(jnp.float32)
        blocks = total.astype(wire) if n + 1 < len(stages) else total
    return blocks.reshape(rows // devices, cols)


def on_device(mesh, glob_out, byte_ids, out_grad, embed, w_proj, norm_gain, w_qkv, w_out):
    vocab, width = embed.shape
    scale = HEAD ** (-0.5)
    gathered = lax.all_to_all(glob_out, "tp", split_axis=0, concat_axis=1, tiled=True)
    patches = gathered.shape[0]
    slices = gathered.reshape(-1, width)
    ids = byte_ids.reshape(-1)
    onehot = (ids[:, None] == jnp.arange(vocab, dtype=jnp.int32)[None, :]).astype(jnp.bfloat16)
    x = jnp.dot(onehot, embed, preferred_element_type=jnp.float32) + jnp.dot(
        slices, w_proj, preferred_element_type=jnp.float32
    )
    inv = lax.rsqrt(jnp.mean(x * x, axis=1, keepdims=True) + 1e-05)
    normed = x * inv
    act = (normed * norm_gain).astype(jnp.bfloat16)
    qkv = jnp.dot(act, w_qkv, preferred_element_type=jnp.float32).astype(jnp.bfloat16)
    parts = qkv.reshape(patches, PATCH, 3, HEADS, HEAD)
    query = parts[:, :, 0]
    keys = parts[:, :, 1]
    values = parts[:, :, 2]
    causal = jnp.arange(PATCH)[:, None] >= jnp.arange(PATCH)[None, :]
    scores = jnp.einsum("pihd,pjhd->phij", query, keys, preferred_element_type=jnp.float32) * scale
    scores = jnp.where(causal, scores, -1e30)
    peak = jnp.max(scores, axis=-1, keepdims=True)
    expo = jnp.exp(scores - peak)
    probs = expo / jnp.sum(expo, axis=-1, keepdims=True)
    probs_b = probs.astype(jnp.bfloat16)
    context = jnp.einsum("phij,pjhd->pihd", probs_b, values, preferred_element_type=jnp.float32)
    context = context.reshape(-1, width).astype(jnp.bfloat16)
    grad_out = jnp.dot(context.T, out_grad, preferred_element_type=jnp.float32)
    d_context = jnp.dot(out_grad, w_out.T, preferred_element_type=jnp.float32).astype(jnp.bfloat16)
    d_context = d_context.reshape(patches, PATCH, HEADS, HEAD)
    d_probs = jnp.einsum("pihd,pjhd->phij", d_context, values, preferred_element_type=jnp.float32)
    d_scores = probs * (d_probs - jnp.sum(probs * d_probs, axis=-1, keepdims=True)) * scale
    d_scores = jnp.where(causal, d_scores, 0.0).astype(jnp.bfloat16)
    d_query = jnp.einsum("phij,pjhd->pihd", d_scores, keys, preferred_element_type=jnp.float32)
    d_key = jnp.einsum("phij,pihd->pjhd", d_scores, query, preferred_element_type=jnp.float32)
    d_value = jnp.einsum("phij,pihd->pjhd", probs_b, d_context, preferred_element_type=jnp.float32)
    d_qkv = jnp.stack([d_query, d_key, d_value], axis=2).reshape(-1, 3 * width).astype(jnp.bfloat16)
    grad_qkv = jnp.dot(act.T, d_qkv, preferred_element_type=jnp.float32)
    d_act = jnp.dot(d_qkv, w_qkv.T, preferred_element_type=jnp.float32)
    grad_gain = jnp.sum(d_act * normed, axis=0)
    d_normed = d_act * norm_gain
    d_x = out_grad.astype(jnp.float32) + inv * (
        d_normed - normed * jnp.mean(d_normed * normed, axis=1, keepdims=True)
    )
    d_x = d_x.astype(jnp.bfloat16)
    glob_rows = jnp.dot(d_x, w_proj.T, preferred_element_type=jnp.float32).astype(jnp.bfloat16)
    glob_grad = lax.all_to_all(
        glob_rows.reshape(patches, -1), "tp", split_axis=1, concat_axis=0, tiled=True
    )
    grad_embed = jnp.dot(onehot.T, d_x, preferred_element_type=jnp.float32)
    grad_proj = jnp.dot(slices.T, d_x, preferred_element_type=jnp.float32)
    tp_bits, seq_bits = bit_masks(mesh)
    devices = mesh.size
    me = lax.axis_index("seq") * mesh.shape["tp"] + lax.axis_index("tp")
    core, wide = tp_bits[:1], tp_bits[1:]
    xy = [core, wide, seq_bits[:1], seq_bits[1:]]
    yx = [core, seq_bits[:1], wide, seq_bits[1:]]
    grad_out = reduce_scatter(grad_out, xy, me, devices)
    third = grad_qkv.shape[1] // 3
    grad_qkv = jnp.concatenate(
        [
            reduce_scatter(grad_qkv[:, n * third : (n + 1) * third], (yx, xy, yx)[n], me, devices)
            for n in range(3)
        ],
        axis=1,
    )
    grad_proj = reduce_scatter(grad_proj, xy, me, devices)
    grad_embed = reduce_scatter(grad_embed, yx, me, devices)
    grad_gain = reduce_scatter(grad_gain.reshape(-1, 1), xy, me, devices, jnp.float32).reshape(-1)
    return (glob_grad, grad_embed, grad_proj, grad_gain, grad_qkv, grad_out)


def solution(mesh):
    return jax.shard_map(
        functools.partial(on_device, mesh),
        mesh=mesh,
        in_specs=(
            P("seq", "tp"),
            P(("seq", "tp"), None),
            P(("seq", "tp"), None),
            P(),
            P(),
            P(),
            P(),
            P(),
        ),
        out_specs=(
            P("seq", "tp"),
            P(("seq", "tp"), None),
            P(("seq", "tp"), None),
            P(("seq", "tp")),
            P(("seq", "tp"), None),
            P(("seq", "tp"), None),
        ),
        check_vma=False,
    )
```

```python
import functools

import jax
import jax.numpy as jnp
from jax import lax
from jax.experimental import pallas as pl
from jax.experimental.pallas import tpu as pltpu
from jax.sharding import PartitionSpec as P

HEADS = 16
HEAD = 64
PATCH = 8
PAIR = 2 * HEAD
GROUP = 16
AXES = ("seq", "tp")
F32 = jnp.float32
BF16 = jnp.bfloat16
NN = (((1,), (0,)), ((), ()))
NT = (((1,), (1,)), ((), ()))
TN = (((0,), (0,)), ((), ()))


def dot(a, b, dims=NN):
    return lax.dot_general(a, b, dims, preferred_element_type=F32)


def cost(flops, nbytes, transcendentals=0):
    return pl.CostEstimate(
        flops=int(flops), bytes_accessed=int(nbytes), transcendentals=int(transcendentals)
    )


def bit_masks(mesh):
    seq, tp = mesh.shape["seq"], mesh.shape["tp"]
    tp_bits = [1 << b for b in range(tp.bit_length() - 1)]
    seq_bits = [tp << b for b in range(seq.bit_length() - 1)]
    return tp_bits, seq_bits


def spans(bits):
    masks = [0]
    for bit in bits:
        masks = masks + [m ^ bit for m in masks]
    return masks


def scatter_order(stages):
    order = [0]
    for bits in reversed(stages):
        order = [m ^ q for m in spans(bits) for q in order]
    return order


def exchange(block, mask, devices):
    return lax.ppermute(block, AXES, [(d, d ^ mask) for d in range(devices)])


def finish_scatter(parts, stages, devices, wire=BF16):
    for n, bits in enumerate(stages):
        masks = spans(bits)
        got = [parts[0]]
        for part, mask in zip(parts[1:], masks[1:]):
            got.append(exchange(part, mask, devices))
        last = n + 1 == len(stages)
        pieces = 1 if last else len(spans(stages[n + 1]))
        size = parts[0].shape[0] // pieces
        parts = []
        for k in reversed(range(pieces)):
            total = got[0][k * size : (k + 1) * size].astype(F32)
            for other in got[1:]:
                total = total + other[k * size : (k + 1) * size].astype(F32)
            parts.append(total if last else total.astype(wire))
        parts = parts[::-1]
    return parts[0]


def split_scatter(blocks, stages, devices, wire=BF16):
    pieces = len(spans(stages[0]))
    size = blocks.shape[0] // pieces
    parts = [blocks[k * size : (k + 1) * size] for k in range(pieces)]
    return finish_scatter(parts, stages, devices, wire)


def project_kernel(
    place, a_ref, b_ref, onehot_ref, embed_ref, w_proj_ref, gain_ref, w_qkv_ref, *rest, alias
):
    if alias:
        rest = rest[5:]
    slices_ref, normed_ref, inv_ref, act_ref, qkv_ref, x_ref = rest
    step = pl.program_id(0)
    half, width = slices_ref.shape[1], slices_ref.shape[2]
    rows = 4 * half

    @pl.when(step == 0)
    def _():
        for k, src in enumerate((a_ref, b_ref)):
            at = 2 * (place[1] ^ k)
            for h in range(2):
                slices_ref[at + h] = src[:, h * width : (h + 1) * width]
        slices = slices_ref[...].reshape(rows, width)
        onehot = onehot_ref[...].reshape(rows, onehot_ref.shape[2])
        for n in range(0, width, 256):
            x_ref[:, n : n + 256] = dot(onehot, embed_ref[:, n : n + 256]) + dot(
                slices, w_proj_ref[:, n : n + 256]
            )
        for r in range(0, rows, half):
            x = x_ref[r : r + half, :]
            inv = lax.rsqrt(jnp.mean(x * x, axis=1, keepdims=True) + 1e-05)
            normed = x * inv
            normed_ref[r // half] = normed
            inv_ref[r // half] = jnp.broadcast_to(inv, (half, 128))
            act_ref[r // half] = (normed * gain_ref[...]).astype(BF16)

    act = act_ref[...].reshape(rows, width)
    qkv_ref[...] = dot(act, w_qkv_ref[...]).astype(BF16).reshape(4, half, w_qkv_ref.shape[1])


def project(place, first, second, onehot, embed, w_proj, gain, w_qkv, earlier):
    half = onehot.shape[1]
    width = w_proj.shape[0]
    vocab = embed.shape[0]
    outs = [
        jax.ShapeDtypeStruct((PATCH, half, width), BF16),
        jax.ShapeDtypeStruct((PATCH, half, width), F32),
        jax.ShapeDtypeStruct((PATCH, half, 128), F32),
        jax.ShapeDtypeStruct((PATCH, half, width), BF16),
        jax.ShapeDtypeStruct((PATCH, half, 3 * width), BF16),
    ]
    block = 512
    if earlier is None:
        first_spec = pl.BlockSpec((half, 2 * width), lambda n, s: (s[2], 0))
    else:
        first_spec = pl.BlockSpec((half, 2 * width), lambda n, s: (0, 0))
    in_specs = [
        first_spec,
        pl.BlockSpec((half, 2 * width), lambda n, s: (0, 0)),
        pl.BlockSpec((4, half, vocab), lambda n, s: (s[0], 0, 0)),
        pl.BlockSpec((vocab, width), lambda n, s: (0, 0)),
        pl.BlockSpec((width, width), lambda n, s: (0, 0)),
        pl.BlockSpec((1, width), lambda n, s: (0, 0)),
        pl.BlockSpec((width, block), lambda n, s: (0, n)),
    ]
    args = [place, first, second, onehot, embed, w_proj, gain, w_qkv]
    aliases = {}
    if earlier is not None:
        in_specs += [pl.BlockSpec(memory_space=pl.ANY)] * 5
        args += list(earlier)
        aliases = {8 + i: i for i in range(5)}
    out_specs = [
        pl.BlockSpec((4, half, width), lambda n, s: (s[0], 0, 0)),
        pl.BlockSpec((4, half, width), lambda n, s: (s[0], 0, 0)),
        pl.BlockSpec((4, half, 128), lambda n, s: (s[0], 0, 0)),
        pl.BlockSpec((4, half, width), lambda n, s: (s[0], 0, 0)),
        pl.BlockSpec((4, half, block), lambda n, s: (s[0], 0, n)),
    ]
    return pl.pallas_call(
        functools.partial(project_kernel, alias=earlier is not None),
        grid_spec=pltpu.PrefetchScalarGridSpec(
            num_scalar_prefetch=1,
            grid=(3 * width // block,),
            in_specs=in_specs,
            out_specs=out_specs,
            scratch_shapes=[pltpu.VMEM((4 * half, width), F32)],
        ),
        out_shape=outs,
        input_output_aliases=aliases,
        cost_estimate=cost(2 * 4 * half * width * (4 * width + vocab), 16e6),
        name="project",
    )(*args)


def attention_kernel(mask_ref, q_ref, k_ref, v_ref, d_ref, context_ref, d_qkv_ref):
    scale = HEAD ** (-0.5)
    mask = mask_ref[...] > 0.5
    lane = lax.broadcasted_iota(jnp.int32, (PATCH * GROUP, PAIR), 1)
    low = lane < HEAD
    rows = PATCH * GROUP

    def block(ref, g):
        return ref[:, g * GROUP : (g + 1) * GROUP, :].reshape(rows, PAIR)

    def stack(value):
        zero = jnp.zeros_like(value)
        return jnp.concatenate([jnp.where(low, value, zero), jnp.where(low, zero, value)], axis=0)

    def merge(value):
        return jnp.where(low, value[:rows], value[rows:]).astype(BF16).reshape(PATCH, GROUP, PAIR)

    for g in range(q_ref.shape[1] // GROUP):
        at = slice(g * GROUP, (g + 1) * GROUP)
        q, k, v, d = block(q_ref, g), block(k_ref, g), block(v_ref, g), block(d_ref, g)
        q2, d2 = stack(q), stack(d)
        scores = jnp.where(mask, dot(q2, k, NT) * scale, -1e30)
        expo = jnp.exp(scores - jnp.max(scores, axis=1, keepdims=True))
        probs = expo * (1.0 / jnp.sum(expo, axis=1, keepdims=True))
        d_probs = dot(d2, v, NT)
        weighted = probs * d_probs
        d_scores = (weighted - probs * jnp.sum(weighted, axis=1, keepdims=True)) * scale
        d_scores = d_scores.astype(BF16)
        probs = probs.astype(BF16)
        context_ref[:, at, :] = merge(dot(probs, v))
        d_qkv_ref[0, :, at, :] = merge(dot(d_scores, k))
        d_qkv_ref[1, :, at, :] = dot(d_scores, q2, TN).astype(BF16).reshape(PATCH, GROUP, PAIR)
        d_qkv_ref[2, :, at, :] = dot(probs, d2, TN).astype(BF16).reshape(PATCH, GROUP, PAIR)


def attention(mask, qkv, d_context, first, count):
    half, width = d_context.shape[1], d_context.shape[2]
    pairs = width // PAIR
    spec = lambda part: pl.BlockSpec((PATCH, half, PAIR), lambda n: (0, 0, part * pairs + first + n))
    return pl.pallas_call(
        attention_kernel,
        grid=(count,),
        in_specs=[
            pl.BlockSpec(mask.shape, lambda n: (0, 0)),
            spec(0),
            spec(1),
            spec(2),
            spec(0),
        ],
        out_specs=[
            pl.BlockSpec((PATCH, half, PAIR), lambda n: (0, 0, n)),
            pl.BlockSpec((3, PATCH, half, PAIR), lambda n: (0, 0, 0, n)),
        ],
        out_shape=[
            jax.ShapeDtypeStruct((PATCH, half, count * PAIR), BF16),
            jax.ShapeDtypeStruct((3, PATCH, half, count * PAIR), BF16),
        ],
        cost_estimate=cost(count * half / GROUP * 6 * 2 * 256 * 256 * 256, count * 1.6e6),
        name="attention",
    )(mask, qkv, qkv, qkv, d_context)


def grad_kernel(place, *refs, counts, height):
    lhs, (rhs_ref, keep_ref, send_ref, acc_ref) = refs[: len(counts)], refs[len(counts) :]
    rhs = rhs_ref[...].reshape(-1, rhs_ref.shape[-1])
    base = 0
    for ref in lhs:
        tokens, cols = rhs.shape[0], ref.shape[-1]
        left = ref[...].reshape(tokens, cols)
        for m in range(0, cols, 256):
            tile = dot(left[:, m : m + 256], rhs, TN)
            for b in range(0, 256, height):
                at = pl.multiple_of(place[(base + m + b) // height] * height, height)
                acc_ref[pl.ds(at, height), :] = tile[b : b + height]
        base += cols
    half = acc_ref.shape[0] // 2
    keep_ref[...] = acc_ref[:half].astype(BF16)
    send_ref[...] = acc_ref[half:].astype(BF16)


def grad_rows(place, lhs, rhs, devices):
    rows = sum(a.shape[-1] for a in lhs)
    cols = rhs.shape[-1]
    stacked = rhs.ndim == 4
    planes = rhs.shape[0] if stacked else 1
    block = 256
    per = cols // block
    whole = lambda a: pl.BlockSpec(a.shape, lambda n, s: (0,) * a.ndim)
    if stacked:
        rhs_spec = pl.BlockSpec((1,) + rhs.shape[1:3] + (block,), lambda n, s: (n // per, 0, 0, n % per))
    else:
        rhs_spec = pl.BlockSpec(rhs.shape[:-1] + (block,), lambda n, s: (0,) * (rhs.ndim - 1) + (n,))
    tokens = rhs.shape[-2] * rhs.shape[-3]
    out = jax.ShapeDtypeStruct((rows // 2, planes * cols), BF16)
    return pl.pallas_call(
        functools.partial(grad_kernel, counts=[a.shape[-1] for a in lhs], height=rows // devices),
        grid_spec=pltpu.PrefetchScalarGridSpec(
            num_scalar_prefetch=1,
            grid=(planes * per,),
            in_specs=[whole(a) for a in lhs] + [rhs_spec],
            out_specs=[pl.BlockSpec((rows // 2, block), lambda n, s: (0, n))] * 2,
            scratch_shapes=[pltpu.VMEM((rows, block), F32)],
        ),
        out_shape=[out, out],
        cost_estimate=cost(2 * tokens * rows * planes * cols, 2 * rows * planes * cols + 4e6),
        name="grad_rows",
    )(place, *lhs, rhs)


def input_grad_kernel(*refs, chunks):
    d_refs, w_refs = refs[:chunks], refs[chunks : 2 * chunks]
    normed_ref, inv_ref, gain_ref, out_grad_ref, d_x_ref, grad_gain_ref, acc_ref = refs[2 * chunks :]
    step = pl.program_id(0)
    half, width = normed_ref.shape[1], normed_ref.shape[2]
    rows = PATCH * half
    for n in range(0, width, 256):
        total = None
        for d_ref, w_ref in zip(d_refs, w_refs):
            term = dot(d_ref[...].reshape(rows, d_ref.shape[-1]), w_ref[n : n + 256, :], NT)
            total = term if total is None else total + term

        @pl.when(step == 0)
        def _():
            acc_ref[:, n : n + 256] = total

        @pl.when(step > 0)
        def _():
            acc_ref[:, n : n + 256] += total

    @pl.when(step == pl.num_programs(0) - 1)
    def _():
        gain_total = jnp.zeros((1, width), F32)
        for j in range(PATCH):
            d_act = acc_ref[j * half : (j + 1) * half, :]
            normed = normed_ref[j]
            inv = inv_ref[j][:, :1]
            gain_total = gain_total + jnp.sum(d_act * normed, axis=0, keepdims=True)
            d_normed = d_act * gain_ref[...]
            mean = jnp.mean(d_normed * normed, axis=1, keepdims=True)
            d_x = out_grad_ref[j].astype(F32) + inv * (d_normed - normed * mean)
            d_x_ref[j] = d_x.astype(BF16)
        grad_gain_ref[...] = gain_total


def input_grad(d_qkvs, w_qkv, normed, inv, gain, out_grad):
    half, width = normed.shape[1], normed.shape[2]
    chunks = len(d_qkvs)
    cols = [d.shape[-1] for d in d_qkvs]
    d_specs, w_specs, at = [], [], 0
    for c in cols:
        d_specs.append(pl.BlockSpec((1, PATCH, half, c), lambda n: (n, 0, 0, 0)))
        w_specs.append(
            pl.BlockSpec((width, c), lambda n, c=c, at=at: (0, n * (width // c) + at // c))
        )
        at += c
    whole = lambda a: pl.BlockSpec(a.shape, lambda n: (0,) * a.ndim)
    return pl.pallas_call(
        functools.partial(input_grad_kernel, chunks=chunks),
        grid=(3,),
        in_specs=d_specs + w_specs + [whole(normed), whole(inv), whole(gain), whole(out_grad)],
        out_specs=[
            pl.BlockSpec((PATCH, half, width), lambda n: (0, 0, 0)),
            pl.BlockSpec((1, width), lambda n: (0, 0)),
        ],
        out_shape=[
            jax.ShapeDtypeStruct((PATCH, half, width), BF16),
            jax.ShapeDtypeStruct((1, width), F32),
        ],
        scratch_shapes=[pltpu.VMEM((PATCH * half, width), F32)],
        cost_estimate=cost(2 * PATCH * half * width * 3 * width, 20e6),
        name="input_grad",
    )(*d_qkvs, *([w_qkv] * chunks), normed, inv, gain, out_grad)


def back_kernel(place, d_x_ref, w_ref, *outs):
    half, width = d_x_ref.shape[1], d_x_ref.shape[2]
    for k, out in enumerate(outs):
        at = 2 * (place[2] ^ k)
        left = d_x_ref[pl.ds(at, 2)].reshape(2 * half, width)
        for n in range(0, width, 256):
            got = dot(left, w_ref[n : n + 256, :], NT).astype(BF16)
            out[:, n : n + 256] = got[:half]
            out[:, width + n : width + n + 256] = got[half:]


def back(place, d_x, w_proj, tp):
    half, width = d_x.shape[1], d_x.shape[2]
    whole = lambda a: pl.BlockSpec(a.shape, lambda n, s: (0,) * a.ndim)
    out = jax.ShapeDtypeStruct((half, 2 * width), BF16)
    return pl.pallas_call(
        back_kernel,
        grid_spec=pltpu.PrefetchScalarGridSpec(
            num_scalar_prefetch=1,
            grid=(1,),
            in_specs=[whole(d_x), whole(w_proj)],
            out_specs=[whole(out)] * tp,
        ),
        out_shape=[out] * tp,
        cost_estimate=cost(2 * PATCH * half * width * width, 6e6),
        name="back",
    )(place, d_x, w_proj)


def on_device(mesh, glob_out, byte_ids, out_grad, embed, w_proj, norm_gain, w_qkv, w_out):
    vocab, width = embed.shape
    tp, devices = mesh.shape["tp"], mesh.size
    half = byte_ids.shape[0]
    t = lax.axis_index("tp").astype(jnp.int32)
    me = lax.axis_index("seq").astype(jnp.int32) * tp + t
    tp_bits, seq_bits = bit_masks(mesh)
    core, wide = tp_bits[:1], tp_bits[1:]
    xy = [core, wide, seq_bits[:1], seq_bits[1:]]
    yx = [core, seq_bits[:1], wide, seq_bits[1:]]

    arrived = {}
    for k in range(1, tp):
        block = lax.dynamic_slice(glob_out, ((t ^ k) * half, 0), (half, glob_out.shape[1]))
        arrived[k] = exchange(block, k, devices)

    onehot = (byte_ids.T[:, :, None] == jnp.arange(vocab, dtype=jnp.int32)).astype(BF16)
    grads = out_grad.reshape(half, PATCH, width).transpose(1, 0, 2)
    d_context = lax.dot_general(
        grads, w_out, (((2,), (1,)), ((), ())), preferred_element_type=F32
    ).astype(BF16)
    gain = norm_gain.reshape(1, width)

    place = jnp.stack([t >> 1, t & 1, t])
    early = project(place, glob_out, arrived[1], onehot, embed, w_proj, gain, w_qkv, None)
    place = jnp.stack([(t >> 1) ^ 1, t & 1, t])
    slices, normed, inv, act, qkv = project(
        place, arrived[2], arrived[3], onehot, embed, w_proj, gain, w_qkv, early
    )

    row = jnp.arange(2 * PATCH * GROUP)[:, None] % (PATCH * GROUP)
    col = jnp.arange(PATCH * GROUP)[None, :]
    mask = ((row % GROUP == col % GROUP) & (row // GROUP >= col // GROUP)).astype(F32)

    def positions(stages):
        order = scatter_order(stages)
        where = [0] * devices
        for p, q in enumerate(order):
            where[q] = p
        table = jnp.array(where, dtype=jnp.int32)
        return table[jnp.arange(devices, dtype=jnp.int32) ^ me]

    at_xy, at_yx = positions(xy), positions(yx)

    pairs = width // PAIR
    splits = 2
    contexts, d_qkvs, qkv_parts = [], [], []
    for c in range(splits):
        count = pairs // splits
        context, d_qkv = attention(mask, qkv, d_context, c * count, count)
        contexts.append(context)
        d_qkvs.append(d_qkv)
        stages, at = ((xy, at_xy), (yx, at_yx))[c % 2]
        pieces = grad_rows(at, [act], d_qkv, devices)
        qkv_parts.append(finish_scatter(list(pieces), stages, devices))
    grad_out = finish_scatter(list(grad_rows(at_xy, contexts, grads, devices)), xy, devices)

    d_x, grad_gain = input_grad(d_qkvs, w_qkv, normed, inv, gain, grads)
    grad_proj = finish_scatter(list(grad_rows(at_yx, [slices], d_x, devices)), yx, devices)

    own = jnp.stack([t >> 1, t & 1, t])
    rows = back(own, d_x, w_proj, tp)
    glob_grad = jnp.zeros((tp * half, 2 * width), BF16)
    for k in range(tp):
        piece = rows[k] if k == 0 else exchange(rows[k], k, devices)
        glob_grad = lax.dynamic_update_slice(glob_grad, piece, ((t ^ k) * half, 0))

    height = vocab // devices
    owner = (byte_ids.T // height) ^ me
    spot = jnp.zeros_like(owner)
    order = scatter_order(yx)
    for bit in range(devices.bit_length() - 1):
        spot = spot + ((owner >> bit) & 1) * order.index(1 << bit)
    spot = spot * height + byte_ids.T % height
    marks = (spot[:, :, None] == jnp.arange(vocab, dtype=jnp.int32)).astype(BF16)
    grad_embed = lax.dot_general(
        marks, d_x, (((0, 1), (0, 1)), ((), ())), preferred_element_type=F32
    ).astype(BF16)
    grad_embed = split_scatter(grad_embed, yx, devices)

    blocks = grad_gain.reshape(devices, width // devices)
    blocks = blocks[jnp.array(scatter_order(yx), dtype=jnp.int32) ^ me]
    grad_gain = split_scatter(blocks, yx, devices, F32).reshape(-1)

    third = width // splits
    grad_qkv = jnp.concatenate(
        [part[:, n * third : (n + 1) * third] for n in range(3) for part in qkv_parts], axis=1
    )
    return (glob_grad, grad_embed, grad_proj, grad_gain, grad_qkv, grad_out)


def solution(mesh):
    return jax.shard_map(
        functools.partial(on_device, mesh),
        mesh=mesh,
        in_specs=(
            P("seq", "tp"),
            P(AXES, None),
            P(AXES, None),
            P(),
            P(),
            P(),
            P(),
            P(),
        ),
        out_specs=(
            P("seq", "tp"),
            P(AXES, None),
            P(AXES, None),
            P(AXES),
            P(AXES, None),
            P(AXES, None),
        ),
        check_vma=False,
    )
```

```python
import functools

import jax
import jax.numpy as jnp
from jax import lax
from jax.experimental import pallas as pl
from jax.experimental.pallas import tpu as pltpu
from jax.sharding import PartitionSpec as P


HEAD = 64
PATCH = 8
PAIR = 2 * HEAD
GROUP = 16
AXES = ("seq", "tp")
F32 = jnp.float32
BF16 = jnp.bfloat16
NN = (((1,), (0,)), ((), ()))
NT = (((1,), (1,)), ((), ()))
TN = (((0,), (0,)), ((), ()))


def dot(a, b, dims=NN):
    return lax.dot_general(a, b, dims, preferred_element_type=F32)


def cost(flops, nbytes, transcendentals=0):
    return pl.CostEstimate(
        flops=int(flops), bytes_accessed=int(nbytes), transcendentals=int(transcendentals)
    )


def bit_masks(mesh):
    seq, tp = mesh.shape["seq"], mesh.shape["tp"]
    tp_bits = [1 << b for b in range(tp.bit_length() - 1)]
    seq_bits = [tp << b for b in range(seq.bit_length() - 1)]
    return tp_bits, seq_bits


def spans(bits):
    masks = [0]
    for bit in bits:
        masks = masks + [m ^ bit for m in masks]
    return masks


def scatter_order(stages):
    order = [0]
    for bits in reversed(stages):
        order = [m ^ q for m in spans(bits) for q in order]
    return order


def exchange(block, mask, devices):
    return lax.ppermute(block, AXES, [(d, d ^ mask) for d in range(devices)])


def finish_scatter(keep, send, bits, devices):
    for n, bit in enumerate(bits):
        got = exchange(send, bit, devices)
        total = keep.astype(F32) + got.astype(F32)
        if n + 1 == len(bits):
            return total
        total = total.astype(keep.dtype)
        half = keep.shape[0] // 2
        keep, send = total[:half], total[half:]


def combine(pairs, mode="split"):
    if mode == "last":
        return [keep.astype(F32) + got.astype(F32) for keep, got in pairs]
    half = pairs[0][0].shape[0] // 2
    halves = []
    for part in (slice(0, half), slice(half, None)):
        sums = [(k[part].astype(F32) + g[part].astype(F32)).astype(BF16) for k, g in pairs]
        halves.append([jnp.concatenate(sums, axis=1)] if mode == "merge" else sums)
    return list(zip(*halves))


def split_scatter(blocks, bits, devices):
    half = blocks.shape[0] // 2
    return finish_scatter(blocks[:half], blocks[half:], bits, devices)


def project_kernel(
    place, a_ref, b_ref, onehot_ref, embed_ref, w_proj_ref, gain_ref, w_qkv_ref, *rest, alias
):
    if alias:
        rest = rest[5:]
    slices_ref, normed_ref, inv_ref, act_ref, qkv_ref, x_ref = rest
    step = pl.program_id(0)
    groups, four, _, width = slices_ref.shape
    tile = four * GROUP
    rows = groups * tile

    @pl.when(step == 0)
    def _():
        for k, src in enumerate((a_ref, b_ref)):
            at = 2 * (place[1] ^ k)
            for g in range(groups):
                for h in range(2):
                    slices_ref[g, at + h] = src[
                        g * GROUP : (g + 1) * GROUP, h * width : (h + 1) * width
                    ]
        slices = slices_ref[...].reshape(rows, width)
        onehot = onehot_ref[...].reshape(rows, onehot_ref.shape[-1])
        for n in range(0, width, 256):
            x_ref[:, n : n + 256] = dot(onehot, embed_ref[:, n : n + 256]) + dot(
                slices, w_proj_ref[:, n : n + 256]
            )
        for g in range(groups):
            for p in range(four):
                at = g * tile + p * GROUP
                x = x_ref[at : at + GROUP, :]
                inv = lax.rsqrt(jnp.mean(x * x, axis=1, keepdims=True) + 1e-05)
                normed = x * inv
                normed_ref[g, p] = normed
                inv_ref[g, p] = jnp.broadcast_to(inv, (GROUP, 128))
                act_ref[g, p] = (normed * gain_ref[...]).astype(BF16)

    act = act_ref[...].reshape(rows, width)
    qkv_ref[...] = dot(act, w_qkv_ref[...]).astype(BF16).reshape(qkv_ref.shape)


def project(place, first, second, onehot, embed, w_proj, gain, w_qkv, earlier):
    groups = onehot.shape[0]
    half = groups * GROUP
    width = w_proj.shape[0]
    vocab = embed.shape[0]
    four = PATCH // 2
    shape = lambda cols, kind: jax.ShapeDtypeStruct((groups, PATCH, GROUP, cols), kind)
    outs = [
        shape(width, BF16),
        shape(width, F32),
        shape(128, F32),
        shape(width, BF16),
        shape(3 * width, BF16),
    ]
    block = 512
    flip = 0 if earlier is None else 1
    part = lambda cols: pl.BlockSpec(
        (groups, four, GROUP, cols), lambda n, s: (0, s[0] ^ flip, 0, 0)
    )
    first_spec = pl.BlockSpec((half, 2 * width), lambda n, s: (0 if flip else s[2], 0))
    in_specs = [
        first_spec,
        pl.BlockSpec((half, 2 * width), lambda n, s: (0, 0)),
        part(vocab),
        pl.BlockSpec((vocab, width), lambda n, s: (0, 0)),
        pl.BlockSpec((width, width), lambda n, s: (0, 0)),
        pl.BlockSpec((1, width), lambda n, s: (0, 0)),
        pl.BlockSpec((width, block), lambda n, s: (0, n)),
    ]
    args = [place, first, second, onehot, embed, w_proj, gain, w_qkv]
    aliases = {}
    if earlier is not None:
        in_specs += [pl.BlockSpec(memory_space=pl.ANY)] * 5
        args += list(earlier)
        aliases = {8 + i: i for i in range(5)}
    out_specs = [
        part(width),
        part(width),
        part(128),
        part(width),
        pl.BlockSpec((groups, four, GROUP, block), lambda n, s: (0, s[0] ^ flip, 0, n)),
    ]
    return pl.pallas_call(
        functools.partial(project_kernel, alias=earlier is not None),
        grid_spec=pltpu.PrefetchScalarGridSpec(
            num_scalar_prefetch=1,
            grid=(3 * width // block,),
            in_specs=in_specs,
            out_specs=out_specs,
            scratch_shapes=[pltpu.VMEM((four * half, width), F32)],
        ),
        out_shape=outs,
        input_output_aliases=aliases,
        cost_estimate=cost(2 * four * half * width * (4 * width + vocab), 16e6),
        name="project",
    )(*args)


def attention_kernel(q_ref, k_ref, v_ref, d_ref, *rest):
    context_ref, d_qkv_ref, mask_ref = rest[-3:]
    rows = PATCH * GROUP
    scale = HEAD ** (-0.5)

    @pl.when(pl.program_id(0) == 0)
    def _():
        key = lax.broadcasted_iota(jnp.int32, (rows, 2 * rows), 0)
        query = lax.broadcasted_iota(jnp.int32, (rows, 2 * rows), 1) % rows
        seen = (key % GROUP == query % GROUP) & (key // GROUP <= query // GROUP)
        mask_ref[...] = seen.astype(F32)

    low = lax.broadcasted_iota(jnp.int32, (rows, PAIR), 1) < HEAD
    own = mask_ref[:GROUP, :] > 0.5

    def stack(value):
        zero = jnp.zeros_like(value)
        return jnp.concatenate([jnp.where(low, value, zero), jnp.where(low, zero, value)], axis=0)

    split = lambda value: value.reshape(PATCH, GROUP, 2 * rows)
    join = lambda value: value.astype(BF16).reshape(rows, 2 * rows)
    for g in range(q_ref.shape[0]):
        q, k, v, d = (ref[g].reshape(rows, PAIR) for ref in (q_ref, k_ref, v_ref, d_ref))
        q2, d2 = stack(q * jnp.asarray(scale, BF16)), stack(d)
        scores = split(jnp.where(mask_ref[...] > 0.5, dot(k, q2, NT), -1e30))
        expo = jnp.exp(scores - jnp.max(scores, axis=0, keepdims=True))
        total = jnp.sum(expo, axis=0, keepdims=True)
        probs = expo * jnp.where(own, 1.0 / total, 0.0)
        d_probs = split(dot(v, d2, NT))
        d_scores = probs * (d_probs - jnp.sum(probs * d_probs, axis=0, keepdims=True))
        probs, d_scores = join(probs), join(d_scores)
        context = dot(v.T, probs).astype(BF16)
        at = slice(g * rows, (g + 1) * rows)
        context_ref[:HEAD, at] = context[:HEAD, :rows]
        context_ref[HEAD:, at] = context[HEAD:, rows:]
        d_query = dot(d_scores, k * jnp.asarray(scale, BF16), TN)
        d_query = jnp.where(low, d_query[:rows], d_query[rows:])
        for n, grad in enumerate((d_query, dot(d_scores, q2), dot(probs, d2))):
            d_qkv_ref[n, g] = grad.astype(BF16).reshape(PATCH, GROUP, PAIR)


def attention(qkv, d_context, first, count, after=()):
    groups, _, _, width = d_context.shape
    pairs = width // PAIR
    tokens = groups * PATCH * GROUP
    spec = lambda part: pl.BlockSpec(
        (groups, PATCH, GROUP, PAIR), lambda n: (0, 0, 0, part * pairs + first + n)
    )
    return pl.pallas_call(
        attention_kernel,
        grid=(count,),
        in_specs=[spec(0), spec(1), spec(2), spec(0)]
        + [pl.BlockSpec(memory_space=pl.ANY)] * len(after),
        out_specs=[
            pl.BlockSpec((PAIR, tokens), lambda n: (n, 0)),
            pl.BlockSpec((3, groups, PATCH, GROUP, PAIR), lambda n: (0, 0, 0, 0, n)),
        ],
        out_shape=[
            jax.ShapeDtypeStruct((count * PAIR, tokens), BF16),
            jax.ShapeDtypeStruct((3, groups, PATCH, GROUP, count * PAIR), BF16),
        ],
        scratch_shapes=[pltpu.VMEM((PATCH * GROUP, 2 * PATCH * GROUP), F32)],
        cost_estimate=cost(count * groups * 6 * 2 * 256 * 256 * 128, count * 1.6e6),
        name="attention",
    )(qkv, qkv, qkv, d_context, *after)


def turn_rows(lhs, left_ref, orders, place, height):
    tokens = left_ref.shape[2]
    base = 0
    for ref in lhs:
        major = ref.ndim == 2
        cols = ref.shape[0] if major else ref.shape[-1]
        for m in range(0, cols, 256):
            if major:
                turned = ref[m : m + 256, :]
            else:
                turned = ref[..., m : m + 256].reshape(tokens, 256).T
            turned = turned.astype(left_ref.dtype)
            for n, (which, order) in enumerate(orders):
                for b in range(0, 256, height):
                    at = order[(base + m + b) // height] ^ place[which]
                    left_ref[n, pl.ds(pl.multiple_of(at * height, height), height), :] = turned[
                        b : b + height
                    ]
        base += cols


def grad_kernel(place, *refs, sources, orders, height, extra):
    lhs, rhs_ref, rest = refs[:sources], refs[sources], refs[sources + 1 :]
    if extra:
        marks_ref, gain_ref = rest[:2]
        marked_ref, column_ref = rest[-2:]
        rest = rest[:-2]
    left_ref, outs = rest[-1], rest[-1 - 2 * len(orders) : -1]
    _, rows, tokens = left_ref.shape
    step = pl.program_id(0)
    steps = pl.num_programs(0)

    @pl.when(step == 0)
    def _():
        turn_rows(lhs, left_ref, orders, place, height)

    def emit(n, rhs):
        keep_ref, send_ref = outs[2 * n], outs[2 * n + 1]
        for m in range(0, rows, 256):
            tile = dot(left_ref[n, m : m + 256, :].astype(BF16), rhs).astype(BF16)
            if m < rows // 2:
                keep_ref[m : m + 256, :] = tile
            else:
                send_ref[m - rows // 2 : m - rows // 2 + 256, :] = tile

    for n in range(len(orders)):
        blocks = steps // len(orders)
        last = 4 if extra else steps

        @pl.when((step >= n * blocks) & (step < jnp.minimum((n + 1) * blocks, last)))
        def _(n=n):
            emit(n, rhs_ref[...].reshape(tokens, rhs_ref.shape[-1]))

    if extra:
        keep_ref, send_ref = outs[-2:]
        half = rows // 2
        per = marks_ref.shape[-1] * height // rows

        @pl.when(step < 4)
        def _():
            marks = marks_ref[...].reshape(tokens, marks_ref.shape[-1])
            got = dot(marks, rhs_ref[...].reshape(tokens, rhs_ref.shape[-1]), TN)
            for p in range(rows // height):
                at = pl.multiple_of(p * height + step * per, per)
                marked_ref[pl.ds(at, per), :] = got[p * per : (p + 1) * per]

        @pl.when(step == 4)
        def _():
            keep_ref[...] = marked_ref[:half].astype(BF16)
            send_ref[...] = marked_ref[half:].astype(BF16)

        @pl.when(step == 5)
        def _():
            column = jnp.sum(gain_ref[...].T, axis=1, keepdims=True)
            which, order = orders[-1]
            for b in range(0, rows, height):
                at = pl.multiple_of((order[b // height] ^ place[which]) * height, height)
                column_ref[pl.ds(at, height), :] = jnp.broadcast_to(
                    column[b : b + height], (height, 256)
                )
            keep_ref[...] = column_ref[:half].astype(BF16)
            send_ref[...] = column_ref[half:].astype(BF16)


def grad_rows(place, kinds, lhs, rhs, devices, after=(), extra=()):
    rows = sum(a.shape[0] if a.ndim == 2 else a.shape[-1] for a in lhs)
    cols = rhs.shape[-1]
    stacked = rhs.ndim == 5
    planes = rhs.shape[0] if stacked else 1
    block = 256
    per = cols // block
    height = rows // devices
    steps = planes * per + (2 if extra else 0)
    whole = lambda a: pl.BlockSpec(a.shape, lambda n, s: (0,) * a.ndim)
    if stacked:
        rhs_spec = pl.BlockSpec(
            (1,) + rhs.shape[1:4] + (block,), lambda n, s: (n // per, 0, 0, 0, n % per)
        )
    else:
        rhs_spec = pl.BlockSpec(
            rhs.shape[:-1] + (block,), lambda n, s: (0, 0, 0, jnp.minimum(n, per - 1))
        )
    tokens = rhs.shape[-2] * rhs.shape[-3] * rhs.shape[-4]
    each = steps // len(kinds)
    out = jax.ShapeDtypeStruct((rows // 2, each * block), BF16)
    out_specs = []
    for n in range(len(kinds)):
        spec = pl.BlockSpec(
            (rows // 2, block), lambda i, s, n=n: (0, jnp.clip(i - n * each, 0, each - 1))
        )
        out_specs += [spec, spec]
    scratch = [pltpu.VMEM((len(kinds), rows, tokens), F32 if height % 16 else BF16)]
    if extra:
        scratch += [pltpu.VMEM((rows, block), F32), pltpu.VMEM((rows, block), F32)]
    got = pl.pallas_call(
        functools.partial(
            grad_kernel,
            sources=len(lhs),
            orders=[(which, spots(stages, devices)) for which, stages in kinds],
            height=height,
            extra=bool(extra),
        ),
        grid_spec=pltpu.PrefetchScalarGridSpec(
            num_scalar_prefetch=1,
            grid=(steps,),
            in_specs=[whole(a) for a in lhs]
            + [rhs_spec]
            + [whole(a) for a in extra]
            + [pl.BlockSpec(memory_space=pl.ANY)] * len(after),
            out_specs=out_specs,
            scratch_shapes=scratch,
        ),
        out_shape=[out] * (2 * len(kinds)),
        cost_estimate=cost(2 * tokens * rows * steps * block, 2 * rows * steps * block + 4e6),
        name="grad_rows",
    )(place, *lhs, rhs, *extra, *after)
    return [(got[n], got[n + 1]) for n in range(0, len(got), 2)]


def input_grad_kernel(*refs, chunks):
    d_refs, w_refs = refs[:chunks], refs[chunks : 2 * chunks]
    normed_ref, inv_ref, gain_ref, out_grad_ref = refs[2 * chunks : 2 * chunks + 4]
    d_x_ref, grad_gain_ref, acc_ref = refs[-3:]
    step = pl.program_id(0)
    groups, _, _, width = normed_ref.shape
    rows = groups * PATCH * GROUP
    for n in range(0, width, 256):
        total = None
        for d_ref, w_ref in zip(d_refs, w_refs):
            term = dot(d_ref[...].reshape(rows, d_ref.shape[-1]), w_ref[n : n + 256, :], NT)
            total = term if total is None else total + term

        @pl.when(step == 0)
        def _():
            acc_ref[:, n : n + 256] = total

        @pl.when(step > 0)
        def _():
            acc_ref[:, n : n + 256] += total

    @pl.when(step == pl.num_programs(0) - 1)
    def _():
        grad_gain_ref[...] = jnp.zeros_like(grad_gain_ref)

        @pl.loop(0, groups)
        def _(g):
          for p in range(PATCH):
            n = g * PATCH + p
            d_act = acc_ref[pl.ds(pl.multiple_of(n * GROUP, GROUP), GROUP), :]
            normed = normed_ref[g, p]
            inv = inv_ref[g, p][:, :1]
            part = d_act * normed
            grad_gain_ref[...] += part[:8] + part[8:]
            d_normed = d_act * gain_ref[...]
            mean = jnp.mean(part * gain_ref[...], axis=1, keepdims=True)
            d_x = out_grad_ref[g, p].astype(F32) + inv * (d_normed - normed * mean)
            d_x_ref[g, p] = d_x.astype(BF16)


def input_grad(d_qkvs, w_qkv, normed, inv, gain, out_grad, after=()):
    groups, _, _, width = normed.shape
    tokens = groups * PATCH * GROUP
    chunks = len(d_qkvs)
    cols = [d.shape[-1] for d in d_qkvs]
    d_specs, w_specs, at = [], [], 0
    for c in cols:
        d_specs.append(pl.BlockSpec((1, groups, PATCH, GROUP, c), lambda n: (n, 0, 0, 0, 0)))
        w_specs.append(
            pl.BlockSpec((width, c), lambda n, c=c, at=at: (0, n * (width // c) + at // c))
        )
        at += c
    whole = lambda a: pl.BlockSpec(a.shape, lambda n: (0,) * a.ndim)
    return pl.pallas_call(
        functools.partial(input_grad_kernel, chunks=chunks),
        grid=(3,),
        in_specs=d_specs
        + w_specs
        + [whole(normed), whole(inv), whole(gain), whole(out_grad)]
        + [pl.BlockSpec(memory_space=pl.ANY)] * len(after),
        out_specs=[
            pl.BlockSpec(normed.shape, lambda n: (0, 0, 0, 0)),
            pl.BlockSpec((8, width), lambda n: (0, 0)),
        ],
        out_shape=[
            jax.ShapeDtypeStruct(normed.shape, BF16),
            jax.ShapeDtypeStruct((8, width), F32),
        ],
        scratch_shapes=[pltpu.VMEM((tokens, width), F32)],
        cost_estimate=cost(2 * tokens * width * 3 * width, 20e6),
        name="input_grad",
    )(*d_qkvs, *([w_qkv] * chunks), normed, inv, gain, out_grad, *after)


def back_kernel(place, d_x_ref, w_ref, *refs, count):
    outs, moved_ref = refs[-count - 1 : -1], refs[-1]
    groups, _, _, width = d_x_ref.shape
    rows = groups * PATCH * GROUP
    left = d_x_ref[...].reshape(rows, width)
    for n in range(0, width, 256):
        got = dot(left, w_ref[n : n + 256, :], NT).astype(BF16)
        got = got.reshape(groups, PATCH, GROUP, 256)
        for g in range(groups):
            for j in range(PATCH):
                moved_ref[j, g * GROUP : (g + 1) * GROUP, n : n + 256] = got[g, j]
    for k, out in enumerate(outs):
        for h in range(2):
            out[:, h * width : (h + 1) * width] = moved_ref[2 * (place[2] ^ k) + h]


def back(place, d_x, w_proj, tp, after=()):
    groups, _, _, width = d_x.shape
    half = groups * GROUP
    whole = lambda a: pl.BlockSpec(a.shape, lambda n, s: (0,) * a.ndim)
    out = jax.ShapeDtypeStruct((half, 2 * width), BF16)
    return pl.pallas_call(
        functools.partial(back_kernel, count=tp),
        grid_spec=pltpu.PrefetchScalarGridSpec(
            num_scalar_prefetch=1,
            grid=(1,),
            in_specs=[whole(d_x), whole(w_proj)]
            + [pl.BlockSpec(memory_space=pl.ANY)] * len(after),
            out_specs=[whole(out)] * tp,
            scratch_shapes=[pltpu.VMEM((PATCH, half, width), BF16)],
        ),
        out_shape=[out] * tp,
        cost_estimate=cost(2 * PATCH * half * width * width, 6e6),
        name="back",
    )(place, d_x, w_proj, *after)


def spots(stages, devices):
    order = scatter_order(stages)
    where = [0] * devices
    for p, q in enumerate(order):
        where[q] = p
    return where


def spot_of(value, stages, devices):
    where = spots(stages, devices)
    total = jnp.zeros_like(value)
    for bit in range(devices.bit_length() - 1):
        total = total + ((value >> bit) & 1) * where[1 << bit]
    return total


def on_device(mesh, glob_out, byte_ids, out_grad, embed, w_proj, norm_gain, w_qkv, w_out):
    vocab, width = embed.shape
    tp, devices = mesh.shape["tp"], mesh.size
    half = byte_ids.shape[0]
    groups = half // GROUP
    t = lax.axis_index("tp").astype(jnp.int32)
    me = lax.axis_index("seq").astype(jnp.int32) * tp + t
    tp_bits, seq_bits = bit_masks(mesh)
    core, wide = tp_bits[:1], tp_bits[1:]
    xy = [core, wide] + [[bit] for bit in seq_bits]
    yx = [core, seq_bits[:1], wide] + [[bit] for bit in seq_bits[1:]]
    place = jnp.stack(
        [t >> 1, t & 1, t, spot_of(me, xy, devices), spot_of(me, yx, devices)]
    )
    XY, YX = (3, xy), (4, yx)

    arrived = {}
    for k in (2, 3, 1)[: tp - 1]:
        block = lax.dynamic_slice(glob_out, ((t ^ k) * half, 0), (half, glob_out.shape[1]))
        arrived[k] = exchange(block, k, devices)

    ids = byte_ids.reshape(groups, GROUP, PATCH).transpose(0, 2, 1)
    onehot = (ids[..., None] == jnp.arange(vocab, dtype=jnp.int32)).astype(BF16)
    grads = out_grad.reshape(groups, GROUP, PATCH, width).transpose(0, 2, 1, 3)
    d_context = lax.dot_general(
        grads, w_out, (((3,), (1,)), ((), ())), preferred_element_type=F32
    ).astype(BF16)
    gain = norm_gain.reshape(1, width)

    early = project(place, glob_out, arrived[1], onehot, embed, w_proj, gain, w_qkv, None)
    slices, normed, inv, act, qkv = project(
        place, arrived[2], arrived[3], onehot, embed, w_proj, gain, w_qkv, early
    )

    def hop(pairs, masks, mode="split"):
        arrived = []
        for (keep, send), mask in zip(pairs, masks):
            arrived.append((keep, exchange(send, mask, devices)))
        return combine(arrived, mode)

    flat = lambda pairs: [a for pair in pairs for a in pair]
    first, second = core[0], (wide[0], seq_bits[0])
    rest = seq_bits[1:]

    def finish(pairs, n=0):
        for bit in rest[n:-1]:
            pairs = hop(pairs, [bit])
            n += 1
        return hop(pairs, [rest[-1]], "last")[0]

    pairs = width // PAIR
    count = pairs // 2
    context_a, d_qkv_a = attention(qkv, d_context, 0, count)
    one = grad_rows(place, (XY, YX), [act], d_qkv_a, devices)
    context_b, d_qkv_b = attention(qkv, d_context, count, count, flat(one)[:1])
    one = hop(one, (first, first))
    two = grad_rows(place, (XY,), [act], d_qkv_b, devices)
    two = two + grad_rows(place, (YX,), [context_a, context_b], grads, devices, flat(two)[:1])
    one = hop(one, second)
    two = hop(two, (first, first))

    d_x, grad_gain = input_grad((d_qkv_a, d_qkv_b), w_qkv, normed, inv, gain, grads)
    one = hop(one, second[::-1], "merge")
    two = hop(two, second)

    height = vocab // devices
    spot = spot_of((ids // height) ^ me, yx, devices) * height + ids % height
    marks = (spot[..., None] == jnp.arange(vocab, dtype=jnp.int32)).astype(BF16)
    fits = height % 8 == 0 and width == 4 * vocab
    extra = (marks, grad_gain) if fits else ()
    three = grad_rows(place, (XY, YX), [slices], d_x, devices, (), extra)

    rows = back(place, d_x, w_proj, tp, flat(three)[:1])
    glob_grad = jnp.zeros((tp * half, 2 * width), BF16)
    for k in range(tp):
        piece = rows[0]
        if k:
            piece = exchange(rows[k], k, devices)
        glob_grad = lax.dynamic_update_slice(glob_grad, piece, ((t ^ k) * half, 0))

    two = hop(two, second[::-1], "merge")
    three = hop(three, (first, first))
    three = hop(three, second)
    three = hop(three, second[::-1], "merge")
    one, two, three = finish(one), finish(two), finish(three)

    each = width // devices
    if fits:
        grad_proj = three[:, :width]
        marked = three[:, width : width + 256].reshape(4, height, 256)
        grad_embed = marked.transpose(1, 0, 2).reshape(height, width)
        grad_gain = three[:, width + 256]
    else:
        grad_proj = three
        grad_embed = lax.dot_general(
            marks, d_x, (((0, 1, 2), (0, 1, 2)), ((), ())), preferred_element_type=F32
        ).astype(BF16)
        flips = [first, second[1], second[0]] + rest
        grad_embed = split_scatter(grad_embed, flips, devices)
        blocks = jnp.sum(grad_gain, axis=0).reshape(devices, each)
        blocks = blocks[jnp.array(scatter_order(yx), dtype=jnp.int32) ^ me]
        grad_gain = split_scatter(blocks, flips, devices).reshape(-1)

    span = count * PAIR
    grad_out = two[:, 3 * span :]
    grad_qkv = jnp.concatenate(
        [part[:, n * span : (n + 1) * span] for n in range(3) for part in (one, two)], axis=1
    )
    return (glob_grad, grad_embed, grad_proj, grad_gain, grad_qkv, grad_out)


def solution(mesh):
    def body(*args):
        return on_device(mesh, *args)

    return shard(body, mesh)


def shard(body, mesh):
    return jax.shard_map(
        body,
        mesh=mesh,
        in_specs=(
            P("seq", "tp"),
            P(AXES, None),
            P(AXES, None),
            P(),
            P(),
            P(),
            P(),
            P(),
        ),
        out_specs=(
            P("seq", "tp"),
            P(AXES, None),
            P(AXES, None),
            P(AXES),
            P(AXES, None),
            P(AXES, None),
        ),
        check_vma=False,
    )
```

```python
import functools

import jax
import jax.numpy as jnp
from jax import lax
from jax.experimental import pallas as pl
from jax.experimental.pallas import tpu as pltpu
from jax.sharding import PartitionSpec as P


HEAD = 64
PATCH = 8
PAIR = 2 * HEAD
GROUP = 16
AXES = ("seq", "tp")
F32 = jnp.float32
BF16 = jnp.bfloat16
NN = (((1,), (0,)), ((), ()))
NT = (((1,), (1,)), ((), ()))
TN = (((0,), (0,)), ((), ()))


def dot(a, b, dims=NN):
    return lax.dot_general(a, b, dims, preferred_element_type=F32)


def cost(flops, nbytes, transcendentals=0):
    return pl.CostEstimate(
        flops=int(flops), bytes_accessed=int(nbytes), transcendentals=int(transcendentals)
    )


def bit_masks(mesh):
    seq, tp = mesh.shape["seq"], mesh.shape["tp"]
    tp_bits = [1 << b for b in range(tp.bit_length() - 1)]
    seq_bits = [tp << b for b in range(seq.bit_length() - 1)]
    return tp_bits, seq_bits


def spans(bits):
    masks = [0]
    for bit in bits:
        masks = masks + [m ^ bit for m in masks]
    return masks


def scatter_order(stages):
    order = [0]
    for bits in reversed(stages):
        order = [m ^ q for m in spans(bits) for q in order]
    return order


def exchange(block, mask, devices):
    return lax.ppermute(block, AXES, [(d, d ^ mask) for d in range(devices)])


def finish_scatter(keep, send, bits, devices):
    for n, bit in enumerate(bits):
        got = exchange(send, bit, devices)
        total = keep.astype(F32) + got.astype(F32)
        if n + 1 == len(bits):
            return total
        total = total.astype(keep.dtype)
        half = keep.shape[0] // 2
        keep, send = total[:half], total[half:]


def combine(pairs, mode="split"):
    if mode == "last":
        return [keep.astype(F32) + got.astype(F32) for keep, got in pairs]
    half = pairs[0][0].shape[0] // 2
    halves = []
    for part in (slice(0, half), slice(half, None)):
        sums = [(k[part].astype(F32) + g[part].astype(F32)).astype(BF16) for k, g in pairs]
        halves.append([jnp.concatenate(sums, axis=1)] if mode == "merge" else sums)
    return list(zip(*halves))


def split_scatter(blocks, bits, devices):
    half = blocks.shape[0] // 2
    return finish_scatter(blocks[:half], blocks[half:], bits, devices)


def project_kernel(
    place, a_ref, b_ref, onehot_ref, embed_ref, w_proj_ref, gain_ref, w_qkv_ref, *rest, alias
):
    if alias:
        rest = rest[5:]
    slices_ref, normed_ref, inv_ref, act_ref, qkv_ref, x_ref = rest
    step = pl.program_id(0)
    groups, four, _, width = slices_ref.shape
    tile = four * GROUP
    rows = groups * tile

    @pl.when(step == 0)
    def _():
        for k, src in enumerate((a_ref, b_ref)):
            at = 2 * (place[1] ^ k)
            for g in range(groups):
                for h in range(2):
                    slices_ref[g, at + h] = src[
                        g * GROUP : (g + 1) * GROUP, h * width : (h + 1) * width
                    ]
        slices = slices_ref[...].reshape(rows, width)
        onehot = onehot_ref[...].reshape(rows, onehot_ref.shape[-1])
        for n in range(0, width, 256):
            x_ref[:, n : n + 256] = dot(onehot, embed_ref[:, n : n + 256]) + dot(
                slices, w_proj_ref[:, n : n + 256]
            )
        for g in range(groups):
            for p in range(four):
                at = g * tile + p * GROUP
                x = x_ref[at : at + GROUP, :]
                inv = lax.rsqrt(jnp.mean(x * x, axis=1, keepdims=True) + 1e-05)
                normed = x * inv
                normed_ref[g, p] = normed
                inv_ref[g, p] = jnp.broadcast_to(inv, (GROUP, 128))
                act_ref[g, p] = (normed * gain_ref[...]).astype(BF16)

    act = act_ref[...].reshape(rows, width)
    qkv_ref[...] = dot(act, w_qkv_ref[...]).astype(BF16).reshape(qkv_ref.shape)


def project(place, first, second, onehot, embed, w_proj, gain, w_qkv, earlier):
    groups = onehot.shape[0]
    half = groups * GROUP
    width = w_proj.shape[0]
    vocab = embed.shape[0]
    four = PATCH // 2
    shape = lambda cols, kind: jax.ShapeDtypeStruct((groups, PATCH, GROUP, cols), kind)
    outs = [
        shape(width, BF16),
        shape(width, F32),
        shape(128, F32),
        shape(width, BF16),
        shape(3 * width, BF16),
    ]
    block = 512
    flip = 0 if earlier is None else 1
    part = lambda cols: pl.BlockSpec(
        (groups, four, GROUP, cols), lambda n, s: (0, s[0] ^ flip, 0, 0)
    )
    first_spec = pl.BlockSpec((half, 2 * width), lambda n, s: (0 if flip else s[2], 0))
    in_specs = [
        first_spec,
        pl.BlockSpec((half, 2 * width), lambda n, s: (0, 0)),
        part(vocab),
        pl.BlockSpec((vocab, width), lambda n, s: (0, 0)),
        pl.BlockSpec((width, width), lambda n, s: (0, 0)),
        pl.BlockSpec((1, width), lambda n, s: (0, 0)),
        pl.BlockSpec((width, block), lambda n, s: (0, n)),
    ]
    args = [place, first, second, onehot, embed, w_proj, gain, w_qkv]
    aliases = {}
    if earlier is not None:
        in_specs += [pl.BlockSpec(memory_space=pl.ANY)] * 5
        args += list(earlier)
        aliases = {8 + i: i for i in range(5)}
    out_specs = [
        part(width),
        part(width),
        part(128),
        part(width),
        pl.BlockSpec((groups, four, GROUP, block), lambda n, s: (0, s[0] ^ flip, 0, n)),
    ]
    return pl.pallas_call(
        functools.partial(project_kernel, alias=earlier is not None),
        grid_spec=pltpu.PrefetchScalarGridSpec(
            num_scalar_prefetch=1,
            grid=(3 * width // block,),
            in_specs=in_specs,
            out_specs=out_specs,
            scratch_shapes=[pltpu.VMEM((four * half, width), F32)],
        ),
        out_shape=outs,
        input_output_aliases=aliases,
        cost_estimate=cost(2 * four * half * width * (4 * width + vocab), 16e6),
        compiler_params=pltpu.CompilerParams(vmem_limit_bytes=24 << 20),
        name="project",
    )(*args)


def attention_kernel(q_ref, k_ref, v_ref, d_ref, *rest):
    context_ref, d_qkv_ref, mask_ref = rest[-3:]
    rows = PATCH * GROUP
    scale = HEAD ** (-0.5)

    @pl.when(pl.program_id(0) == 0)
    def _():
        key = lax.broadcasted_iota(jnp.int32, (rows, 2 * rows), 0)
        query = lax.broadcasted_iota(jnp.int32, (rows, 2 * rows), 1) % rows
        seen = (key % GROUP == query % GROUP) & (key // GROUP <= query // GROUP)
        mask_ref[...] = seen.astype(F32)

    low = lax.broadcasted_iota(jnp.int32, (rows, PAIR), 1) < HEAD
    own = mask_ref[:GROUP, :] > 0.5

    def stack(value):
        zero = jnp.zeros_like(value)
        return jnp.concatenate([jnp.where(low, value, zero), jnp.where(low, zero, value)], axis=0)

    split = lambda value: value.reshape(PATCH, GROUP, 2 * rows)
    join = lambda value: value.astype(BF16).reshape(rows, 2 * rows)
    for g in range(q_ref.shape[0]):
        q, k, v, d = (ref[g].reshape(rows, PAIR) for ref in (q_ref, k_ref, v_ref, d_ref))
        q2, d2 = stack(q * jnp.asarray(scale, BF16)), stack(d)
        scores = split(jnp.where(mask_ref[...] > 0.5, dot(k, q2, NT), -1e30))
        expo = jnp.exp(scores - jnp.max(scores, axis=0, keepdims=True))
        total = jnp.sum(expo, axis=0, keepdims=True)
        probs = expo * jnp.where(own, 1.0 / total, 0.0)
        d_probs = split(dot(v, d2, NT))
        d_scores = probs * (d_probs - jnp.sum(probs * d_probs, axis=0, keepdims=True))
        probs, d_scores = join(probs), join(d_scores)
        context = dot(v.T, probs).astype(BF16)
        at = slice(g * rows, (g + 1) * rows)
        context_ref[:HEAD, at] = context[:HEAD, :rows]
        context_ref[HEAD:, at] = context[HEAD:, rows:]
        d_query = dot(d_scores, k * jnp.asarray(scale, BF16), TN)
        d_query = jnp.where(low, d_query[:rows], d_query[rows:])
        for n, grad in enumerate((d_query, dot(d_scores, q2), dot(probs, d2))):
            d_qkv_ref[n, g] = grad.astype(BF16).reshape(PATCH, GROUP, PAIR)


def attention(qkv, d_context, first, count, after=()):
    groups, _, _, width = d_context.shape
    pairs = width // PAIR
    tokens = groups * PATCH * GROUP
    spec = lambda part: pl.BlockSpec(
        (groups, PATCH, GROUP, PAIR), lambda n: (0, 0, 0, part * pairs + first + n)
    )
    return pl.pallas_call(
        attention_kernel,
        grid=(count,),
        in_specs=[spec(0), spec(1), spec(2), spec(0)]
        + [pl.BlockSpec(memory_space=pl.ANY)] * len(after),
        out_specs=[
            pl.BlockSpec((PAIR, tokens), lambda n: (n, 0)),
            pl.BlockSpec((3, groups, PATCH, GROUP, PAIR), lambda n: (0, 0, 0, 0, n)),
        ],
        out_shape=[
            jax.ShapeDtypeStruct((count * PAIR, tokens), BF16),
            jax.ShapeDtypeStruct((3, groups, PATCH, GROUP, count * PAIR), BF16),
        ],
        scratch_shapes=[pltpu.VMEM((PATCH * GROUP, 2 * PATCH * GROUP), F32)],
        cost_estimate=cost(count * groups * 6 * 2 * 256 * 256 * 128, count * 1.6e6),
        compiler_params=pltpu.CompilerParams(vmem_limit_bytes=12 << 20),
        name="attention",
    )(qkv, qkv, qkv, d_context, *after)


def turn_rows(lhs, left_ref, orders, place, height):
    tokens = left_ref.shape[2]
    base = 0
    for ref in lhs:
        major = ref.ndim == 2
        cols = ref.shape[0] if major else ref.shape[-1]
        for m in range(0, cols, 256):
            if major:
                turned = ref[m : m + 256, :]
            else:
                turned = ref[..., m : m + 256].reshape(tokens, 256).T
            turned = turned.astype(left_ref.dtype)
            for n, (which, order) in enumerate(orders):
                for b in range(0, 256, height):
                    at = order[(base + m + b) // height] ^ place[which]
                    left_ref[n, pl.ds(pl.multiple_of(at * height, height), height), :] = turned[
                        b : b + height
                    ]
        base += cols


def grad_kernel(place, *refs, sources, orders, height, extra):
    lhs, rhs_ref, rest = refs[:sources], refs[sources], refs[sources + 1 :]
    if extra:
        marks_ref, gain_ref = rest[:2]
        marked_ref, column_ref = rest[-2:]
        rest = rest[:-2]
    left_ref, outs = rest[-1], rest[-1 - 2 * len(orders) : -1]
    _, rows, tokens = left_ref.shape
    step = pl.program_id(0)
    steps = pl.num_programs(0)

    @pl.when(step == 0)
    def _():
        turn_rows(lhs, left_ref, orders, place, height)

    def emit(n, rhs):
        keep_ref, send_ref = outs[2 * n], outs[2 * n + 1]
        for m in range(0, rows, 256):
            tile = dot(left_ref[n, m : m + 256, :].astype(BF16), rhs).astype(BF16)
            if m < rows // 2:
                keep_ref[m : m + 256, :] = tile
            else:
                send_ref[m - rows // 2 : m - rows // 2 + 256, :] = tile

    for n in range(len(orders)):
        blocks = steps // len(orders)
        last = 4 if extra else steps

        @pl.when((step >= n * blocks) & (step < jnp.minimum((n + 1) * blocks, last)))
        def _(n=n):
            emit(n, rhs_ref[...].reshape(tokens, rhs_ref.shape[-1]))

    if extra:
        keep_ref, send_ref = outs[-2:]
        half = rows // 2
        per = marks_ref.shape[-1] * height // rows

        @pl.when(step < 4)
        def _():
            marks = marks_ref[...].reshape(tokens, marks_ref.shape[-1])
            got = dot(marks, rhs_ref[...].reshape(tokens, rhs_ref.shape[-1]), TN)
            for p in range(rows // height):
                at = pl.multiple_of(p * height + step * per, per)
                marked_ref[pl.ds(at, per), :] = got[p * per : (p + 1) * per]

        @pl.when(step == 4)
        def _():
            keep_ref[...] = marked_ref[:half].astype(BF16)
            send_ref[...] = marked_ref[half:].astype(BF16)

        @pl.when(step == 5)
        def _():
            column = jnp.sum(gain_ref[...].T, axis=1, keepdims=True)
            which, order = orders[-1]
            for b in range(0, rows, height):
                at = pl.multiple_of((order[b // height] ^ place[which]) * height, height)
                column_ref[pl.ds(at, height), :] = jnp.broadcast_to(
                    column[b : b + height], (height, 256)
                )
            keep_ref[...] = column_ref[:half].astype(BF16)
            send_ref[...] = column_ref[half:].astype(BF16)


def grad_rows(place, kinds, lhs, rhs, devices, after=(), extra=()):
    rows = sum(a.shape[0] if a.ndim == 2 else a.shape[-1] for a in lhs)
    cols = rhs.shape[-1]
    stacked = rhs.ndim == 5
    planes = rhs.shape[0] if stacked else 1
    block = 256
    per = cols // block
    height = rows // devices
    steps = planes * per + (2 if extra else 0)
    whole = lambda a: pl.BlockSpec(a.shape, lambda n, s: (0,) * a.ndim)
    if stacked:
        rhs_spec = pl.BlockSpec(
            (1,) + rhs.shape[1:4] + (block,), lambda n, s: (n // per, 0, 0, 0, n % per)
        )
    else:
        rhs_spec = pl.BlockSpec(
            rhs.shape[:-1] + (block,), lambda n, s: (0, 0, 0, jnp.minimum(n, per - 1))
        )
    tokens = rhs.shape[-2] * rhs.shape[-3] * rhs.shape[-4]
    each = steps // len(kinds)
    out = jax.ShapeDtypeStruct((rows // 2, each * block), BF16)
    out_specs = []
    for n in range(len(kinds)):
        spec = pl.BlockSpec(
            (rows // 2, block), lambda i, s, n=n: (0, jnp.clip(i - n * each, 0, each - 1))
        )
        out_specs += [spec, spec]
    scratch = [pltpu.VMEM((len(kinds), rows, tokens), F32 if height % 16 else BF16)]
    if extra:
        scratch += [pltpu.VMEM((rows, block), F32), pltpu.VMEM((rows, block), F32)]
    got = pl.pallas_call(
        functools.partial(
            grad_kernel,
            sources=len(lhs),
            orders=[(which, spots(stages, devices)) for which, stages in kinds],
            height=height,
            extra=bool(extra),
        ),
        grid_spec=pltpu.PrefetchScalarGridSpec(
            num_scalar_prefetch=1,
            grid=(steps,),
            in_specs=[whole(a) for a in lhs]
            + [rhs_spec]
            + [whole(a) for a in extra]
            + [pl.BlockSpec(memory_space=pl.ANY)] * len(after),
            out_specs=out_specs,
            scratch_shapes=scratch,
        ),
        out_shape=[out] * (2 * len(kinds)),
        cost_estimate=cost(2 * tokens * rows * steps * block, 2 * rows * steps * block + 4e6),
        compiler_params=pltpu.CompilerParams(vmem_limit_bytes=20 << 20),
        name="grad_rows",
    )(place, *lhs, rhs, *extra, *after)
    return [(got[n], got[n + 1]) for n in range(0, len(got), 2)]


def input_grad_kernel(*refs, chunks):
    d_refs, w_refs = refs[:chunks], refs[chunks : 2 * chunks]
    normed_ref, inv_ref, gain_ref, out_grad_ref = refs[2 * chunks : 2 * chunks + 4]
    d_x_ref, grad_gain_ref, acc_ref = refs[-3:]
    step = pl.program_id(0)
    groups, _, _, width = normed_ref.shape
    rows = groups * PATCH * GROUP
    for n in range(0, width, 256):
        total = None
        for d_ref, w_ref in zip(d_refs, w_refs):
            term = dot(d_ref[...].reshape(rows, d_ref.shape[-1]), w_ref[n : n + 256, :], NT)
            total = term if total is None else total + term

        @pl.when(step == 0)
        def _():
            acc_ref[:, n : n + 256] = total

        @pl.when(step > 0)
        def _():
            acc_ref[:, n : n + 256] += total

    @pl.when(step == pl.num_programs(0) - 1)
    def _():
        grad_gain_ref[...] = jnp.zeros_like(grad_gain_ref)

        @pl.loop(0, groups)
        def _(g):
          for p in range(PATCH):
            n = g * PATCH + p
            d_act = acc_ref[pl.ds(pl.multiple_of(n * GROUP, GROUP), GROUP), :]
            normed = normed_ref[g, p]
            inv = inv_ref[g, p][:, :1]
            part = d_act * normed
            grad_gain_ref[...] += part[:8] + part[8:]
            d_normed = d_act * gain_ref[...]
            mean = jnp.mean(part * gain_ref[...], axis=1, keepdims=True)
            d_x = out_grad_ref[g, p].astype(F32) + inv * (d_normed - normed * mean)
            d_x_ref[g, p] = d_x.astype(BF16)


def input_grad(d_qkvs, w_qkv, normed, inv, gain, out_grad, after=()):
    groups, _, _, width = normed.shape
    tokens = groups * PATCH * GROUP
    chunks = len(d_qkvs)
    cols = [d.shape[-1] for d in d_qkvs]
    d_specs, w_specs, at = [], [], 0
    for c in cols:
        d_specs.append(pl.BlockSpec((1, groups, PATCH, GROUP, c), lambda n: (n, 0, 0, 0, 0)))
        w_specs.append(
            pl.BlockSpec((width, c), lambda n, c=c, at=at: (0, n * (width // c) + at // c))
        )
        at += c
    whole = lambda a: pl.BlockSpec(a.shape, lambda n: (0,) * a.ndim)
    return pl.pallas_call(
        functools.partial(input_grad_kernel, chunks=chunks),
        grid=(3,),
        in_specs=d_specs
        + w_specs
        + [whole(normed), whole(inv), whole(gain), whole(out_grad)]
        + [pl.BlockSpec(memory_space=pl.ANY)] * len(after),
        out_specs=[
            pl.BlockSpec(normed.shape, lambda n: (0, 0, 0, 0)),
            pl.BlockSpec((8, width), lambda n: (0, 0)),
        ],
        out_shape=[
            jax.ShapeDtypeStruct(normed.shape, BF16),
            jax.ShapeDtypeStruct((8, width), F32),
        ],
        scratch_shapes=[pltpu.VMEM((tokens, width), F32)],
        cost_estimate=cost(2 * tokens * width * 3 * width, 20e6),
        compiler_params=pltpu.CompilerParams(vmem_limit_bytes=28 << 20),
        name="input_grad",
    )(*d_qkvs, *([w_qkv] * chunks), normed, inv, gain, out_grad, *after)


def back_kernel(place, d_x_ref, w_ref, *refs, count):
    outs, moved_ref = refs[-count - 1 : -1], refs[-1]
    groups, _, _, width = d_x_ref.shape
    rows = groups * PATCH * GROUP
    left = d_x_ref[...].reshape(rows, width)
    for n in range(0, width, 256):
        got = dot(left, w_ref[n : n + 256, :], NT).astype(BF16)
        got = got.reshape(groups, PATCH, GROUP, 256)
        for g in range(groups):
            for j in range(PATCH):
                moved_ref[j, g * GROUP : (g + 1) * GROUP, n : n + 256] = got[g, j]
    for k, out in enumerate(outs):
        for h in range(2):
            out[:, h * width : (h + 1) * width] = moved_ref[2 * (place[2] ^ k) + h]


def back(place, d_x, w_proj, tp, after=()):
    groups, _, _, width = d_x.shape
    half = groups * GROUP
    whole = lambda a: pl.BlockSpec(a.shape, lambda n, s: (0,) * a.ndim)
    out = jax.ShapeDtypeStruct((half, 2 * width), BF16)
    return pl.pallas_call(
        functools.partial(back_kernel, count=tp),
        grid_spec=pltpu.PrefetchScalarGridSpec(
            num_scalar_prefetch=1,
            grid=(1,),
            in_specs=[whole(d_x), whole(w_proj)]
            + [pl.BlockSpec(memory_space=pl.ANY)] * len(after),
            out_specs=[whole(out)] * tp,
            scratch_shapes=[pltpu.VMEM((PATCH, half, width), BF16)],
        ),
        out_shape=[out] * tp,
        cost_estimate=cost(2 * PATCH * half * width * width, 6e6),
        compiler_params=pltpu.CompilerParams(vmem_limit_bytes=16 << 20),
        name="back",
    )(place, d_x, w_proj, *after)


def spots(stages, devices):
    order = scatter_order(stages)
    where = [0] * devices
    for p, q in enumerate(order):
        where[q] = p
    return where


def spot_of(value, stages, devices):
    where = spots(stages, devices)
    total = jnp.zeros_like(value)
    for bit in range(devices.bit_length() - 1):
        total = total + ((value >> bit) & 1) * where[1 << bit]
    return total


def on_device(mesh, glob_out, byte_ids, out_grad, embed, w_proj, norm_gain, w_qkv, w_out):
    vocab, width = embed.shape
    tp, devices = mesh.shape["tp"], mesh.size
    half = byte_ids.shape[0]
    groups = half // GROUP
    t = lax.axis_index("tp").astype(jnp.int32)
    me = lax.axis_index("seq").astype(jnp.int32) * tp + t
    tp_bits, seq_bits = bit_masks(mesh)
    core, wide = tp_bits[:1], tp_bits[1:]
    xy = [core, wide] + [[bit] for bit in seq_bits]
    yx = [core, seq_bits[:1], wide] + [[bit] for bit in seq_bits[1:]]
    place = jnp.stack(
        [t >> 1, t & 1, t, spot_of(me, xy, devices), spot_of(me, yx, devices)]
    )
    XY, YX = (3, xy), (4, yx)

    arrived = {}
    for k in (2, 3, 1)[: tp - 1]:
        block = lax.dynamic_slice(glob_out, ((t ^ k) * half, 0), (half, glob_out.shape[1]))
        arrived[k] = exchange(block, k, devices)

    ids = byte_ids.reshape(groups, GROUP, PATCH).transpose(0, 2, 1)
    onehot = (ids[..., None] == jnp.arange(vocab, dtype=jnp.int32)).astype(BF16)
    grads = out_grad.reshape(groups, GROUP, PATCH, width).transpose(0, 2, 1, 3)
    d_context = lax.dot_general(
        grads, w_out, (((3,), (1,)), ((), ())), preferred_element_type=F32
    ).astype(BF16)
    gain = norm_gain.reshape(1, width)

    early = project(place, glob_out, arrived[1], onehot, embed, w_proj, gain, w_qkv, None)
    slices, normed, inv, act, qkv = project(
        place, arrived[2], arrived[3], onehot, embed, w_proj, gain, w_qkv, early
    )

    def hop(pairs, masks, mode="split"):
        arrived = []
        for (keep, send), mask in zip(pairs, masks):
            arrived.append((keep, exchange(send, mask, devices)))
        return combine(arrived, mode)

    flat = lambda pairs: [a for pair in pairs for a in pair]
    first, second = core[0], (wide[0], seq_bits[0])
    rest = seq_bits[1:]

    def finish(pairs, n=0):
        for bit in rest[n:-1]:
            pairs = hop(pairs, [bit])
            n += 1
        return hop(pairs, [rest[-1]], "last")[0]

    pairs = width // PAIR
    count = pairs // 2
    context_a, d_qkv_a = attention(qkv, d_context, 0, count)
    one = grad_rows(place, (XY, YX), [act], d_qkv_a, devices)
    context_b, d_qkv_b = attention(qkv, d_context, count, count, flat(one)[:1])
    one = hop(one, (first, first))
    two = grad_rows(place, (XY,), [act], d_qkv_b, devices)
    two = two + grad_rows(place, (YX,), [context_a, context_b], grads, devices, flat(two)[:1])
    one = hop(one, second)
    two = hop(two, (first, first))

    d_x, grad_gain = input_grad((d_qkv_a, d_qkv_b), w_qkv, normed, inv, gain, grads)
    one = hop(one, second[::-1], "merge")
    two = hop(two, second)

    height = vocab // devices
    spot = spot_of((ids // height) ^ me, yx, devices) * height + ids % height
    marks = (spot[..., None] == jnp.arange(vocab, dtype=jnp.int32)).astype(BF16)
    fits = height % 8 == 0 and width == 4 * vocab
    extra = (marks, grad_gain) if fits else ()
    three = grad_rows(place, (XY, YX), [slices], d_x, devices, (), extra)

    rows = back(place, d_x, w_proj, tp, flat(three)[:1])
    glob_grad = jnp.zeros((tp * half, 2 * width), BF16)
    for k in range(tp):
        piece = rows[0]
        if k:
            piece = exchange(rows[k], k, devices)
        glob_grad = lax.dynamic_update_slice(glob_grad, piece, ((t ^ k) * half, 0))

    two = hop(two, second[::-1], "merge")
    three = hop(three, (first, first))
    three = hop(three, second)
    three = hop(three, second[::-1], "merge")
    one, two, three = finish(one), finish(two), finish(three)

    each = width // devices
    if fits:
        grad_proj = three[:, :width]
        marked = three[:, width : width + 256].reshape(4, height, 256)
        grad_embed = marked.transpose(1, 0, 2).reshape(height, width)
        grad_gain = three[:, width + 256]
    else:
        grad_proj = three
        grad_embed = lax.dot_general(
            marks, d_x, (((0, 1, 2), (0, 1, 2)), ((), ())), preferred_element_type=F32
        ).astype(BF16)
        flips = [first, second[1], second[0]] + rest
        grad_embed = split_scatter(grad_embed, flips, devices)
        blocks = jnp.sum(grad_gain, axis=0).reshape(devices, each)
        blocks = blocks[jnp.array(scatter_order(yx), dtype=jnp.int32) ^ me]
        grad_gain = split_scatter(blocks, flips, devices).reshape(-1)

    span = count * PAIR
    grad_out = two[:, 3 * span :]
    grad_qkv = jnp.concatenate(
        [part[:, n * span : (n + 1) * span] for n in range(3) for part in (one, two)], axis=1
    )
    return (glob_grad, grad_embed, grad_proj, grad_gain, grad_qkv, grad_out)


def solution(mesh):
    def body(*args):
        return on_device(mesh, *args)

    return shard(body, mesh)


def shard(body, mesh):
    return jax.shard_map(
        body,
        mesh=mesh,
        in_specs=(
            P("seq", "tp"),
            P(AXES, None),
            P(AXES, None),
            P(),
            P(),
            P(),
            P(),
            P(),
        ),
        out_specs=(
            P("seq", "tp"),
            P(AXES, None),
            P(AXES, None),
            P(AXES),
            P(AXES, None),
            P(AXES, None),
        ),
        check_vma=False,
    )
```

```python
import functools

import jax
import jax.numpy as jnp
from jax import lax
from jax.experimental import pallas as pl
from jax.experimental.pallas import tpu as pltpu
from jax.sharding import PartitionSpec as P


HEAD = 64
PATCH = 8
PAIR = 2 * HEAD
GROUP = 16
AXES = ("seq", "tp")
F32 = jnp.float32
BF16 = jnp.bfloat16
NN = (((1,), (0,)), ((), ()))
NT = (((1,), (1,)), ((), ()))
TN = (((0,), (0,)), ((), ()))


def dot(a, b, dims=NN):
    return lax.dot_general(a, b, dims, preferred_element_type=F32)


def cost(flops, nbytes, transcendentals=0):
    return pl.CostEstimate(
        flops=int(flops), bytes_accessed=int(nbytes), transcendentals=int(transcendentals)
    )


def bit_masks(mesh):
    seq, tp = mesh.shape["seq"], mesh.shape["tp"]
    tp_bits = [1 << b for b in range(tp.bit_length() - 1)]
    seq_bits = [tp << b for b in range(seq.bit_length() - 1)]
    return tp_bits, seq_bits


def spans(bits):
    masks = [0]
    for bit in bits:
        masks = masks + [m ^ bit for m in masks]
    return masks


def scatter_order(stages):
    order = [0]
    for bits in reversed(stages):
        order = [m ^ q for m in spans(bits) for q in order]
    return order


def exchange(block, mask, devices):
    return lax.ppermute(block, AXES, [(d, d ^ mask) for d in range(devices)])


def finish_scatter(keep, send, bits, devices):
    for n, bit in enumerate(bits):
        got = exchange(send, bit, devices)
        total = keep.astype(F32) + got.astype(F32)
        if n + 1 == len(bits):
            return total
        total = total.astype(keep.dtype)
        half = keep.shape[0] // 2
        keep, send = total[:half], total[half:]


def combine(pairs, mode="split"):
    if mode == "last":
        return [keep.astype(F32) + got.astype(F32) for keep, got in pairs]
    half = pairs[0][0].shape[0] // 2
    halves = []
    for part in (slice(0, half), slice(half, None)):
        sums = [(k[part].astype(F32) + g[part].astype(F32)).astype(BF16) for k, g in pairs]
        halves.append([jnp.concatenate(sums, axis=1)] if mode == "merge" else sums)
    return list(zip(*halves))


def split_scatter(blocks, bits, devices):
    half = blocks.shape[0] // 2
    return finish_scatter(blocks[:half], blocks[half:], bits, devices)


def project_kernel(
    place, a_ref, b_ref, onehot_ref, embed_ref, w_proj_ref, gain_ref, w_qkv_ref, *rest, alias
):
    if alias:
        rest = rest[5:]
    slices_ref, normed_ref, inv_ref, act_ref, qkv_ref, x_ref = rest
    step = pl.program_id(0)
    groups, four, _, width = slices_ref.shape
    tile = four * GROUP
    rows = groups * tile

    @pl.when(step == 0)
    def _():
        for k, src in enumerate((a_ref, b_ref)):
            at = 2 * (place[1] ^ k)
            for g in range(groups):
                for h in range(2):
                    slices_ref[g, at + h] = src[
                        g * GROUP : (g + 1) * GROUP, h * width : (h + 1) * width
                    ]
        slices = slices_ref[...].reshape(rows, width)
        onehot = onehot_ref[...].reshape(rows, onehot_ref.shape[-1])
        for n in range(0, width, 256):
            x_ref[:, n : n + 256] = dot(onehot, embed_ref[:, n : n + 256]) + dot(
                slices, w_proj_ref[:, n : n + 256]
            )
        tiles = [slice(c, c + 128) for c in range(0, width, 128)]
        for g in range(groups):
            for p in range(four):
                at = slice(g * tile + p * GROUP, g * tile + (p + 1) * GROUP)
                square = jnp.zeros((GROUP, 128), F32)
                for c in tiles:
                    square = square + x_ref[at, c] * x_ref[at, c]
                mean = jnp.sum(square, axis=1, keepdims=True) * (1.0 / width)
                inv = jnp.broadcast_to(lax.rsqrt(mean + 1e-05), (GROUP, 128))
                inv_ref[g, p] = inv
                for c in tiles:
                    normed = x_ref[at, c] * inv
                    normed_ref[g, p, :, c] = normed
                    act_ref[g, p, :, c] = (normed * gain_ref[:, c]).astype(BF16)

    act = act_ref[...].reshape(rows, width)
    qkv_ref[...] = dot(act, w_qkv_ref[...]).astype(BF16).reshape(qkv_ref.shape)


def project(place, first, second, onehot, embed, w_proj, gain, w_qkv, earlier):
    groups = onehot.shape[0]
    half = groups * GROUP
    width = w_proj.shape[0]
    vocab = embed.shape[0]
    four = PATCH // 2
    shape = lambda cols, kind: jax.ShapeDtypeStruct((groups, PATCH, GROUP, cols), kind)
    outs = [
        shape(width, BF16),
        shape(width, F32),
        shape(128, F32),
        shape(width, BF16),
        shape(3 * width, BF16),
    ]
    block = 512
    flip = 0 if earlier is None else 1
    once = pl.Buffered(1)
    part = lambda cols: pl.BlockSpec(
        (groups, four, GROUP, cols), lambda n, s: (0, s[0] ^ flip, 0, 0), pipeline_mode=once
    )
    first_spec = pl.BlockSpec(
        (half, 2 * width), lambda n, s: (0 if flip else s[2], 0), pipeline_mode=once
    )
    in_specs = [
        first_spec,
        pl.BlockSpec((half, 2 * width), lambda n, s: (0, 0), pipeline_mode=once),
        part(vocab),
        pl.BlockSpec((vocab, width), lambda n, s: (0, 0), pipeline_mode=once),
        pl.BlockSpec((width, width), lambda n, s: (0, 0), pipeline_mode=once),
        pl.BlockSpec((1, width), lambda n, s: (0, 0), pipeline_mode=once),
        pl.BlockSpec((width, block), lambda n, s: (0, n)),
    ]
    keep = lambda a: pltpu.with_memory_space_constraint(a, pltpu.HBM)
    first = first if flip else keep(first)
    args = [place, first, second, onehot, embed, keep(w_proj), gain, keep(w_qkv)]
    aliases = {}
    if earlier is not None:
        in_specs += [pl.BlockSpec(memory_space=pl.ANY)] * 5
        args += list(earlier)
        aliases = {8 + i: i for i in range(5)}
    out_specs = [
        part(width),
        part(width),
        part(128),
        part(width),
        pl.BlockSpec((groups, four, GROUP, block), lambda n, s: (0, s[0] ^ flip, 0, n)),
    ]
    return pl.pallas_call(
        functools.partial(project_kernel, alias=earlier is not None),
        grid_spec=pltpu.PrefetchScalarGridSpec(
            num_scalar_prefetch=1,
            grid=(3 * width // block,),
            in_specs=in_specs,
            out_specs=out_specs,
            scratch_shapes=[pltpu.VMEM((four * half, width), F32)],
        ),
        out_shape=outs,
        input_output_aliases=aliases,
        cost_estimate=cost(2 * four * half * width * (4 * width + vocab), 16e6),
        compiler_params=pltpu.CompilerParams(vmem_limit_bytes=16 << 20),
        name="project",
    )(*args)


def attention_kernel(q_ref, k_ref, v_ref, d_ref, *rest):
    context_ref, d_qkv_ref, bias_ref, own_ref, s_ref, dp_ref, p_ref, ds_ref = rest[-8:]
    rows = PATCH * GROUP
    groups = q_ref.shape[0]
    scale = jnp.asarray(HEAD ** (-0.5), BF16)

    @pl.when(pl.program_id(0) == 0)
    def _():
        key = lax.broadcasted_iota(jnp.int32, (rows, rows), 0)
        query = lax.broadcasted_iota(jnp.int32, (rows, rows), 1)
        same = key % GROUP == query % GROUP
        bias_ref[...] = jnp.where(same & (key // GROUP <= query // GROUP), 0.0, -1e30)
        own_ref[...] = same[:GROUP].astype(F32)

    low = lax.broadcasted_iota(jnp.int32, (rows, PAIR), 1) < HEAD

    def stack(value):
        zero = jnp.zeros_like(value)
        return jnp.concatenate([jnp.where(low, value, zero), jnp.where(low, zero, value)], axis=0)

    block = lambda ref, g: ref[g].reshape(rows, PAIR)
    for g in range(groups):
        s_ref[g] = dot(block(k_ref, g), stack(block(q_ref, g) * scale), NT)
        dp_ref[g] = dot(block(v_ref, g), stack(block(d_ref, g)), NT)
    for g in range(groups):
        for h in range(2):
            at = slice(h * rows, (h + 1) * rows)
            scores = (s_ref[g, :, at] + bias_ref[...]).reshape(PATCH, GROUP, rows)
            expo = jnp.exp(scores - jnp.max(scores, axis=0, keepdims=True))
            total = jnp.sum(expo, axis=0, keepdims=True)
            probs = expo * (own_ref[...] / total)
            d_probs = dp_ref[g, :, at].reshape(PATCH, GROUP, rows)
            d_scores = probs * (d_probs - jnp.sum(probs * d_probs, axis=0, keepdims=True))
            p_ref[g, :, at] = probs.astype(BF16).reshape(rows, rows)
            ds_ref[g, :, at] = d_scores.astype(BF16).reshape(rows, rows)
    for g in range(groups):
        k = block(k_ref, g)
        probs, d_scores = p_ref[g], ds_ref[g]
        context = dot(block(v_ref, g).T, probs).astype(BF16)
        at = slice(g * rows, (g + 1) * rows)
        context_ref[:HEAD, at] = context[:HEAD, :rows]
        context_ref[HEAD:, at] = context[HEAD:, rows:]
        d_query = dot(d_scores, k * scale, TN)
        d_query = jnp.where(low, d_query[:rows], d_query[rows:])
        d_key = dot(d_scores, stack(block(q_ref, g) * scale))
        d_value = dot(probs, stack(block(d_ref, g)))
        for n, grad in enumerate((d_query, d_key, d_value)):
            d_qkv_ref[n, g] = grad.astype(BF16).reshape(PATCH, GROUP, PAIR)


def attention(qkv, d_context, first, count, after=()):
    groups, _, _, width = d_context.shape
    pairs = width // PAIR
    tokens = groups * PATCH * GROUP
    spec = lambda part: pl.BlockSpec(
        (groups, PATCH, GROUP, PAIR), lambda n: (0, 0, 0, part * pairs + first + n)
    )
    return pl.pallas_call(
        attention_kernel,
        grid=(count,),
        in_specs=[spec(0), spec(1), spec(2), spec(0)]
        + [pl.BlockSpec(memory_space=pl.ANY)] * len(after),
        out_specs=[
            pl.BlockSpec((PAIR, tokens), lambda n: (n, 0)),
            pl.BlockSpec((3, groups, PATCH, GROUP, PAIR), lambda n: (0, 0, 0, 0, n)),
        ],
        out_shape=[
            jax.ShapeDtypeStruct((count * PAIR, tokens), BF16),
            jax.ShapeDtypeStruct((3, groups, PATCH, GROUP, count * PAIR), BF16),
        ],
        scratch_shapes=[
            pltpu.VMEM((PATCH * GROUP, PATCH * GROUP), F32),
            pltpu.VMEM((GROUP, PATCH * GROUP), F32),
            pltpu.VMEM((groups, PATCH * GROUP, 2 * PATCH * GROUP), F32),
            pltpu.VMEM((groups, PATCH * GROUP, 2 * PATCH * GROUP), F32),
            pltpu.VMEM((groups, PATCH * GROUP, 2 * PATCH * GROUP), BF16),
            pltpu.VMEM((groups, PATCH * GROUP, 2 * PATCH * GROUP), BF16),
        ],
        cost_estimate=cost(count * groups * 6 * 2 * 256 * 256 * 128, count * 1.6e6),
        compiler_params=pltpu.CompilerParams(vmem_limit_bytes=11 << 20),
        name="attention",
    )(qkv, qkv, qkv, d_context, *after)


def turn_rows(lhs, left_ref, orders, place, height):
    tokens = left_ref.shape[2]
    base = 0
    for ref in lhs:
        major = ref.ndim == 2
        cols = ref.shape[0] if major else ref.shape[-1]
        for m in range(0, cols, 256):
            if major:
                turned = ref[m : m + 256, :]
            else:
                turned = ref[..., m : m + 256].reshape(tokens, 256).T
            turned = turned.astype(left_ref.dtype)
            for n, (which, order) in enumerate(orders):
                for b in range(0, 256, height):
                    at = order[(base + m + b) // height] ^ place[which]
                    left_ref[n, pl.ds(pl.multiple_of(at * height, height), height), :] = turned[
                        b : b + height
                    ]
        base += cols


def grad_kernel(place, *refs, sources, orders, height, extra):
    lhs, rhs_ref, rest = refs[:sources], refs[sources], refs[sources + 1 :]
    if extra:
        marks_ref, gain_ref = rest[:2]
        marked_ref, column_ref = rest[-2:]
        rest = rest[:-2]
    left_ref, outs = rest[-1], rest[-1 - 2 * len(orders) : -1]
    _, rows, tokens = left_ref.shape
    step = pl.program_id(0)
    steps = pl.num_programs(0)

    @pl.when(step == 0)
    def _():
        turn_rows(lhs, left_ref, orders, place, height)

    def emit(n, rhs):
        keep_ref, send_ref = outs[2 * n], outs[2 * n + 1]
        for m in range(0, rows, 256):
            tile = dot(left_ref[n, m : m + 256, :].astype(BF16), rhs).astype(BF16)
            if m < rows // 2:
                keep_ref[m : m + 256, :] = tile
            else:
                send_ref[m - rows // 2 : m - rows // 2 + 256, :] = tile

    for n in range(len(orders)):
        blocks = steps // len(orders)
        last = 4 if extra else steps

        @pl.when((step >= n * blocks) & (step < jnp.minimum((n + 1) * blocks, last)))
        def _(n=n):
            emit(n, rhs_ref[...].reshape(tokens, rhs_ref.shape[-1]))

    if extra:
        keep_ref, send_ref = outs[-2:]
        half = rows // 2
        per = marks_ref.shape[-1] * height // rows

        @pl.when(step < 4)
        def _():
            marks = marks_ref[...].reshape(tokens, marks_ref.shape[-1])
            got = dot(marks, rhs_ref[...].reshape(tokens, rhs_ref.shape[-1]), TN)
            for p in range(rows // height):
                at = pl.multiple_of(p * height + step * per, per)
                marked_ref[pl.ds(at, per), :] = got[p * per : (p + 1) * per]

        @pl.when(step == 4)
        def _():
            keep_ref[...] = marked_ref[:half].astype(BF16)
            send_ref[...] = marked_ref[half:].astype(BF16)

        @pl.when(step == 5)
        def _():
            column = jnp.sum(gain_ref[...].T, axis=1, keepdims=True)
            which, order = orders[-1]
            for b in range(0, rows, height):
                at = pl.multiple_of((order[b // height] ^ place[which]) * height, height)
                column_ref[pl.ds(at, height), :] = jnp.broadcast_to(
                    column[b : b + height], (height, 256)
                )
            keep_ref[...] = column_ref[:half].astype(BF16)
            send_ref[...] = column_ref[half:].astype(BF16)


def grad_rows(place, kinds, lhs, rhs, devices, after=(), extra=()):
    rows = sum(a.shape[0] if a.ndim == 2 else a.shape[-1] for a in lhs)
    cols = rhs.shape[-1]
    stacked = rhs.ndim == 5
    planes = rhs.shape[0] if stacked else 1
    block = 256
    per = cols // block
    height = rows // devices
    steps = planes * per + (2 if extra else 0)
    whole = lambda a: pl.BlockSpec(
        a.shape, lambda n, s: (0,) * a.ndim, pipeline_mode=pl.Buffered(1)
    )
    if stacked:
        rhs_spec = pl.BlockSpec(
            (1,) + rhs.shape[1:4] + (block,), lambda n, s: (n // per, 0, 0, 0, n % per)
        )
    else:
        rhs_spec = pl.BlockSpec(
            rhs.shape[:-1] + (block,), lambda n, s: (0, 0, 0, jnp.minimum(n, per - 1))
        )
    tokens = rhs.shape[-2] * rhs.shape[-3] * rhs.shape[-4]
    each = steps // len(kinds)
    out = jax.ShapeDtypeStruct((rows // 2, each * block), BF16)
    out_specs = []
    for n in range(len(kinds)):
        spec = pl.BlockSpec(
            (rows // 2, block), lambda i, s, n=n: (0, jnp.clip(i - n * each, 0, each - 1))
        )
        out_specs += [spec, spec]
    scratch = [pltpu.VMEM((len(kinds), rows, tokens), F32 if height % 16 else BF16)]
    if extra:
        scratch += [pltpu.VMEM((rows, block), F32), pltpu.VMEM((rows, block), F32)]
    got = pl.pallas_call(
        functools.partial(
            grad_kernel,
            sources=len(lhs),
            orders=[(which, spots(stages, devices)) for which, stages in kinds],
            height=height,
            extra=bool(extra),
        ),
        grid_spec=pltpu.PrefetchScalarGridSpec(
            num_scalar_prefetch=1,
            grid=(steps,),
            in_specs=[whole(a) for a in lhs]
            + [rhs_spec]
            + [whole(a) for a in extra]
            + [pl.BlockSpec(memory_space=pl.ANY)] * len(after),
            out_specs=out_specs,
            scratch_shapes=scratch,
        ),
        out_shape=[out] * (2 * len(kinds)),
        cost_estimate=cost(2 * tokens * rows * steps * block, 2 * rows * steps * block + 4e6),
        compiler_params=pltpu.CompilerParams(vmem_limit_bytes=13 << 20),
        name="grad_rows",
    )(place, *lhs, rhs, *extra, *after)
    return [(got[n], got[n + 1]) for n in range(0, len(got), 2)]


def input_grad_kernel(*refs, chunks):
    d_refs, w_refs = refs[:chunks], refs[chunks : 2 * chunks]
    normed_ref, inv_ref, gain_ref, out_grad_ref = refs[2 * chunks : 2 * chunks + 4]
    d_x_ref, grad_gain_ref, acc_ref = refs[-3:]
    step = pl.program_id(0)
    groups, _, _, width = normed_ref.shape
    rows = groups * PATCH * GROUP
    for n in range(0, width, 256):
        total = None
        for d_ref, w_ref in zip(d_refs, w_refs):
            term = dot(d_ref[...].reshape(rows, d_ref.shape[-1]), w_ref[n : n + 256, :], NT)
            total = term if total is None else total + term

        @pl.when(step == 0)
        def _():
            acc_ref[:, n : n + 256] = total

        @pl.when(step > 0)
        def _():
            acc_ref[:, n : n + 256] += total

    @pl.when(step == pl.num_programs(0) - 1)
    def _():
        grad_gain_ref[...] = jnp.zeros_like(grad_gain_ref)
        tiles = [slice(c, c + 128) for c in range(0, width, 128)]

        @pl.loop(0, groups)
        def _(g):
            at = [pl.multiple_of((g * PATCH + p) * GROUP, GROUP) for p in range(PATCH)]
            sums = [jnp.zeros((GROUP, 128), F32) for _ in range(PATCH)]
            for tile in tiles:
                total = jnp.zeros((GROUP, 128), F32)
                for p in range(PATCH):
                    part = acc_ref[pl.ds(at[p], GROUP), tile] * normed_ref[g, p, :, tile]
                    total = total + part
                    sums[p] = sums[p] + part * gain_ref[:, tile]
                grad_gain_ref[:, tile] += total[:8] + total[8:]
            for p in range(PATCH):
                mean = jnp.sum(sums[p], axis=1, keepdims=True) * (1.0 / width)
                inv = inv_ref[g, p]
                for tile in tiles:
                    d_normed = acc_ref[pl.ds(at[p], GROUP), tile] * gain_ref[:, tile]
                    d_x = inv * (d_normed - normed_ref[g, p, :, tile] * mean)
                    d_x = out_grad_ref[g, p, :, tile].astype(F32) + d_x
                    d_x_ref[g, p, :, tile] = d_x.astype(BF16)


def input_grad(d_qkvs, w_qkv, normed, inv, gain, out_grad, after=()):
    groups, _, _, width = normed.shape
    tokens = groups * PATCH * GROUP
    chunks = len(d_qkvs)
    cols = [d.shape[-1] for d in d_qkvs]
    d_specs, w_specs, at = [], [], 0
    for c in cols:
        d_specs.append(pl.BlockSpec((1, groups, PATCH, GROUP, c), lambda n: (n, 0, 0, 0, 0)))
        w_specs.append(
            pl.BlockSpec((width, c), lambda n, c=c, at=at: (0, n * (width // c) + at // c))
        )
        at += c
    whole = lambda a: pl.BlockSpec(
        a.shape, lambda n: (0,) * a.ndim, pipeline_mode=pl.Buffered(1)
    )
    return pl.pallas_call(
        functools.partial(input_grad_kernel, chunks=chunks),
        grid=(3,),
        in_specs=d_specs
        + w_specs
        + [whole(normed), whole(inv), whole(gain), whole(out_grad)]
        + [pl.BlockSpec(memory_space=pl.ANY)] * len(after),
        out_specs=[
            pl.BlockSpec(normed.shape, lambda n: (0, 0, 0, 0)),
            pl.BlockSpec((8, width), lambda n: (0, 0)),
        ],
        out_shape=[
            jax.ShapeDtypeStruct(normed.shape, BF16),
            jax.ShapeDtypeStruct((8, width), F32),
        ],
        scratch_shapes=[pltpu.VMEM((tokens, width), F32)],
        cost_estimate=cost(2 * tokens * width * 3 * width, 20e6),
        compiler_params=pltpu.CompilerParams(vmem_limit_bytes=20 << 20),
        name="input_grad",
    )(*d_qkvs, *([w_qkv] * chunks), normed, inv, gain, out_grad, *after)


def back_kernel(place, d_x_ref, w_ref, *refs, count):
    outs, moved_ref = refs[-count - 1 : -1], refs[-1]
    groups, _, _, width = d_x_ref.shape
    rows = groups * PATCH * GROUP
    left = d_x_ref[...].reshape(rows, width)
    for n in range(0, width, 256):
        got = dot(left, w_ref[n : n + 256, :], NT).astype(BF16)
        got = got.reshape(groups, PATCH, GROUP, 256)
        for g in range(groups):
            for j in range(PATCH):
                moved_ref[j, g * GROUP : (g + 1) * GROUP, n : n + 256] = got[g, j]
    for k, out in enumerate(outs):
        for h in range(2):
            out[:, h * width : (h + 1) * width] = moved_ref[2 * (place[2] ^ k) + h]


def back(place, d_x, w_proj, tp, after=()):
    groups, _, _, width = d_x.shape
    half = groups * GROUP
    whole = lambda a: pl.BlockSpec(
        a.shape, lambda n, s: (0,) * a.ndim, pipeline_mode=pl.Buffered(1)
    )
    out = jax.ShapeDtypeStruct((half, 2 * width), BF16)
    return pl.pallas_call(
        functools.partial(back_kernel, count=tp),
        grid_spec=pltpu.PrefetchScalarGridSpec(
            num_scalar_prefetch=1,
            grid=(1,),
            in_specs=[whole(d_x), whole(w_proj)]
            + [pl.BlockSpec(memory_space=pl.ANY)] * len(after),
            out_specs=[whole(out)] * tp,
            scratch_shapes=[pltpu.VMEM((PATCH, half, width), BF16)],
        ),
        out_shape=[out] * tp,
        cost_estimate=cost(2 * PATCH * half * width * width, 6e6),
        compiler_params=pltpu.CompilerParams(vmem_limit_bytes=11 << 20),
        name="back",
    )(place, d_x, w_proj, *after)


def spots(stages, devices):
    order = scatter_order(stages)
    where = [0] * devices
    for p, q in enumerate(order):
        where[q] = p
    return where


def spot_of(value, stages, devices):
    where = spots(stages, devices)
    total = jnp.zeros_like(value)
    for bit in range(devices.bit_length() - 1):
        total = total + ((value >> bit) & 1) * where[1 << bit]
    return total


def on_device(mesh, glob_out, byte_ids, out_grad, embed, w_proj, norm_gain, w_qkv, w_out):
    vocab, width = embed.shape
    tp, devices = mesh.shape["tp"], mesh.size
    half = byte_ids.shape[0]
    groups = half // GROUP
    t = lax.axis_index("tp").astype(jnp.int32)
    me = lax.axis_index("seq").astype(jnp.int32) * tp + t
    tp_bits, seq_bits = bit_masks(mesh)
    core, wide = tp_bits[:1], tp_bits[1:]
    xy = [core, wide] + [[bit] for bit in seq_bits]
    yx = [core, seq_bits[:1], wide] + [[bit] for bit in seq_bits[1:]]
    yzx = [core] + [[bit] for bit in seq_bits] + [wide]
    place = jnp.stack([t >> 1, t & 1, t] + [spot_of(me, o, devices) for o in (xy, yx, yzx)])
    XY, YX, YZX = (3, xy), (4, yx), (5, yzx)

    arrived = {}
    for k in (2, 3, 1)[: tp - 1]:
        block = lax.dynamic_slice(glob_out, ((t ^ k) * half, 0), (half, glob_out.shape[1]))
        arrived[k] = exchange(block, k, devices)

    ids = byte_ids.reshape(groups, GROUP, PATCH).transpose(0, 2, 1)
    onehot = (ids[..., None] == jnp.arange(vocab, dtype=jnp.int32)).astype(BF16)
    grads = out_grad.reshape(groups, GROUP, PATCH, width).transpose(0, 2, 1, 3)
    d_context = lax.dot_general(
        grads, w_out, (((3,), (1,)), ((), ())), preferred_element_type=F32
    ).astype(BF16)
    gain = norm_gain.reshape(1, width)

    early = project(place, glob_out, arrived[1], onehot, embed, w_proj, gain, w_qkv, None)
    slices, normed, inv, act, qkv = project(
        place, arrived[2], arrived[3], onehot, embed, w_proj, gain, w_qkv, early
    )

    def hop(pairs, masks, mode="split"):
        arrived = []
        for (keep, send), mask in zip(pairs, masks):
            arrived.append((keep, exchange(send, mask, devices)))
        return combine(arrived, mode)

    flat = lambda pairs: [a for pair in pairs for a in pair]
    first, second = core[0], (wide[0], seq_bits[0])
    rest = seq_bits[1:]

    def finish(pairs, n=0):
        for bit in rest[n:-1]:
            pairs = hop(pairs, [bit])
            n += 1
        return hop(pairs, [rest[-1]], "last")[0]

    pairs = width // PAIR
    count = pairs // 2
    context_a, d_qkv_a = attention(qkv, d_context, 0, count)
    one = grad_rows(place, (XY, YX), [act], d_qkv_a, devices)
    context_b, d_qkv_b = attention(qkv, d_context, count, count, flat(one)[:1])
    one = hop(one, (first, first))
    two = grad_rows(place, (XY,), [act], d_qkv_b, devices)
    two = two + grad_rows(place, (YX,), [context_a, context_b], grads, devices, flat(two)[:1])
    one = hop(one, second)
    two = hop(two, (first, first))

    d_x, grad_gain = input_grad((d_qkv_a, d_qkv_b), w_qkv, normed, inv, gain, grads)
    one = hop(one, second[::-1], "merge")
    two = hop(two, second)

    height = vocab // devices
    spot = spot_of((ids // height) ^ me, yzx, devices) * height + ids % height
    marks = (spot[..., None] == jnp.arange(vocab, dtype=jnp.int32)).astype(BF16)
    fits = height % 8 == 0 and width == 4 * vocab
    extra = (marks, grad_gain) if fits else ()
    three = grad_rows(place, (XY, YZX), [slices], d_x, devices, (), extra)

    rows = back(place, d_x, w_proj, tp, flat(three)[:1])
    glob_grad = jnp.zeros((tp * half, 2 * width), BF16)
    for k in range(tp):
        piece = rows[0]
        if k:
            piece = exchange(rows[k], k, devices)
        glob_grad = lax.dynamic_update_slice(glob_grad, piece, ((t ^ k) * half, 0))

    two = hop(two, second[::-1], "merge")
    three = hop(three, (first, first))
    paths = list(zip([b[0] for b in xy[1:]], [b[0] for b in yzx[1:]]))
    for n, masks in enumerate(paths):
        last = n + 1 == len(paths)
        three = hop(three, masks, "last" if last else "split")
    one, two = finish(one), finish(two)

    each = width // devices
    if fits:
        cut = width - three[0].shape[1]
        grad_proj = jnp.concatenate([three[0], three[1][:, :cut]], axis=1)
        marked = three[1][:, cut : cut + 256].reshape(4, height, 256)
        grad_embed = marked.transpose(1, 0, 2).reshape(height, width)
        grad_gain = three[1][:, cut + 256]
    else:
        grad_proj = jnp.concatenate(three, axis=1)
        grad_embed = lax.dot_general(
            marks, d_x, (((0, 1, 2), (0, 1, 2)), ((), ())), preferred_element_type=F32
        ).astype(BF16)
        flips = [b[0] for b in yzx]
        grad_embed = split_scatter(grad_embed, flips, devices)
        blocks = jnp.sum(grad_gain, axis=0).reshape(devices, each)
        blocks = blocks[jnp.array(scatter_order(yzx), dtype=jnp.int32) ^ me]
        grad_gain = split_scatter(blocks, flips, devices).reshape(-1)

    span = count * PAIR
    grad_out = two[:, 3 * span :]
    grad_qkv = jnp.concatenate(
        [part[:, n * span : (n + 1) * span] for n in range(3) for part in (one, two)], axis=1
    )
    return (glob_grad, grad_embed, grad_proj, grad_gain, grad_qkv, grad_out)


def solution(mesh):
    def body(*args):
        return on_device(mesh, *args)

    return shard(body, mesh)


def shard(body, mesh):
    return jax.shard_map(
        body,
        mesh=mesh,
        in_specs=(
            P("seq", "tp"),
            P(AXES, None),
            P(AXES, None),
            P(),
            P(),
            P(),
            P(),
            P(),
        ),
        out_specs=(
            P("seq", "tp"),
            P(AXES, None),
            P(AXES, None),
            P(AXES),
            P(AXES, None),
            P(AXES, None),
        ),
        check_vma=False,
    )
```

```python
import functools

import jax
import jax.numpy as jnp
from jax import lax
from jax.experimental import pallas as pl
from jax.experimental.pallas import tpu as pltpu
from jax.sharding import PartitionSpec as P


HEAD = 64
PATCH = 8
PAIR = 2 * HEAD
GROUP = 16
AXES = ("seq", "tp")
F32 = jnp.float32
BF16 = jnp.bfloat16
NN = (((1,), (0,)), ((), ()))
NT = (((1,), (1,)), ((), ()))
TN = (((0,), (0,)), ((), ()))


def dot(a, b, dims=NN):
    return lax.dot_general(a, b, dims, preferred_element_type=F32)


def cost(flops, nbytes, transcendentals=0):
    return pl.CostEstimate(
        flops=int(flops), bytes_accessed=int(nbytes), transcendentals=int(transcendentals)
    )


def in_hbm(value):
    return pltpu.with_memory_space_constraint(value, pltpu.HBM)


def bit_masks(mesh):
    seq, tp = mesh.shape["seq"], mesh.shape["tp"]
    tp_bits = [1 << b for b in range(tp.bit_length() - 1)]
    seq_bits = [tp << b for b in range(seq.bit_length() - 1)]
    return tp_bits, seq_bits


def spans(bits):
    masks = [0]
    for bit in bits:
        masks = masks + [m ^ bit for m in masks]
    return masks


def scatter_order(stages):
    order = [0]
    for bits in reversed(stages):
        order = [m ^ q for m in spans(bits) for q in order]
    return order


def exchange(block, mask, devices):
    return lax.ppermute(block, AXES, [(d, d ^ mask) for d in range(devices)])


def finish_scatter(keep, send, bits, devices):
    for n, bit in enumerate(bits):
        got = exchange(send, bit, devices)
        total = keep.astype(F32) + got.astype(F32)
        if n + 1 == len(bits):
            return total
        total = total.astype(keep.dtype)
        half = keep.shape[0] // 2
        keep, send = total[:half], total[half:]


def combine(pairs, mode="split"):
    if mode == "last":
        return [keep.astype(F32) + got.astype(F32) for keep, got in pairs]
    half = pairs[0][0].shape[0] // 2
    halves = []
    for part in (slice(0, half), slice(half, None)):
        sums = [(k[part].astype(F32) + g[part].astype(F32)).astype(BF16) for k, g in pairs]
        halves.append([jnp.concatenate(sums, axis=1)] if mode == "merge" else sums)
    return list(zip(*halves))


def split_scatter(blocks, bits, devices):
    half = blocks.shape[0] // 2
    return finish_scatter(blocks[:half], blocks[half:], bits, devices)


def project_kernel(
    place, a_ref, b_ref, onehot_ref, embed_ref, w_proj_ref, gain_ref, w_qkv_ref, *rest, alias
):
    if alias:
        rest = rest[5:]
    slices_ref, normed_ref, inv_ref, act_ref, qkv_ref, x_ref = rest
    step = pl.program_id(0)
    groups, four, _, width = slices_ref.shape
    tile = four * GROUP
    rows = groups * tile

    @pl.when(step == 0)
    def _():
        for k, src in enumerate((a_ref, b_ref)):
            at = 2 * (place[1] ^ k)
            for g in range(groups):
                for h in range(2):
                    slices_ref[g, at + h] = src[
                        g * GROUP : (g + 1) * GROUP, h * width : (h + 1) * width
                    ]
        slices = slices_ref[...].reshape(rows, width)
        onehot = onehot_ref[...].reshape(rows, onehot_ref.shape[-1])
        for n in range(0, width, 256):
            x_ref[:, n : n + 256] = dot(onehot, embed_ref[:, n : n + 256]) + dot(
                slices, w_proj_ref[:, n : n + 256]
            )
        tiles = [slice(c, c + 128) for c in range(0, width, 128)]
        for g in range(groups):
            for p in range(four):
                at = slice(g * tile + p * GROUP, g * tile + (p + 1) * GROUP)
                square = jnp.zeros((GROUP, 128), F32)
                for c in tiles:
                    square = square + x_ref[at, c] * x_ref[at, c]
                mean = jnp.sum(square, axis=1, keepdims=True) * (1.0 / width)
                inv = jnp.broadcast_to(lax.rsqrt(mean + 1e-05), (GROUP, 128))
                inv_ref[g, p] = inv
                for c in tiles:
                    normed = x_ref[at, c] * inv
                    normed_ref[g, p, :, c] = normed
                    act_ref[g, p, :, c] = (normed * gain_ref[:, c]).astype(BF16)

    act = act_ref[...].reshape(rows, width)
    qkv_ref[...] = dot(act, w_qkv_ref[...]).astype(BF16).reshape(qkv_ref.shape)


def project(place, first, second, onehot, embed, w_proj, gain, w_qkv, earlier):
    groups = onehot.shape[0]
    half = groups * GROUP
    width = w_proj.shape[0]
    vocab = embed.shape[0]
    four = PATCH // 2
    shape = lambda cols, kind: jax.ShapeDtypeStruct((groups, PATCH, GROUP, cols), kind)
    outs = [
        shape(width, BF16),
        shape(width, F32),
        shape(128, F32),
        shape(width, BF16),
        shape(3 * width, BF16),
    ]
    block = 512
    flip = 0 if earlier is None else 1
    once = pl.Buffered(1)
    part = lambda cols: pl.BlockSpec(
        (groups, four, GROUP, cols), lambda n, s: (0, s[0] ^ flip, 0, 0), pipeline_mode=once
    )
    first_spec = pl.BlockSpec(
        (half, 2 * width), lambda n, s: (0 if flip else s[2], 0), pipeline_mode=once
    )
    in_specs = [
        first_spec,
        pl.BlockSpec((half, 2 * width), lambda n, s: (0, 0), pipeline_mode=once),
        part(vocab),
        pl.BlockSpec((vocab, width), lambda n, s: (0, 0), pipeline_mode=once),
        pl.BlockSpec((width, width), lambda n, s: (0, 0), pipeline_mode=once),
        pl.BlockSpec((1, width), lambda n, s: (0, 0), pipeline_mode=once),
        pl.BlockSpec((width, block), lambda n, s: (0, n)),
    ]
    first = first if flip else in_hbm(first)
    args = [place, first, second, onehot, embed, in_hbm(w_proj), gain, in_hbm(w_qkv)]
    aliases = {}
    if earlier is not None:
        in_specs += [pl.BlockSpec(memory_space=pl.ANY)] * 5
        args += list(earlier)
        aliases = {8 + i: i for i in range(5)}
    out_specs = [
        part(width),
        part(width),
        part(128),
        part(width),
        pl.BlockSpec((groups, four, GROUP, block), lambda n, s: (0, s[0] ^ flip, 0, n)),
    ]
    return pl.pallas_call(
        functools.partial(project_kernel, alias=earlier is not None),
        grid_spec=pltpu.PrefetchScalarGridSpec(
            num_scalar_prefetch=1,
            grid=(3 * width // block,),
            in_specs=in_specs,
            out_specs=out_specs,
            scratch_shapes=[pltpu.VMEM((four * half, width), F32)],
        ),
        out_shape=outs,
        input_output_aliases=aliases,
        cost_estimate=cost(2 * four * half * width * (4 * width + vocab), 16e6),
        compiler_params=pltpu.CompilerParams(vmem_limit_bytes=16 << 20),
        name="project",
    )(*args)


def attention_kernel(q_ref, k_ref, v_ref, d_ref, *rest):
    context_ref, d_qkv_ref, bias_ref, own_ref, s_ref, dp_ref, p_ref, ds_ref = rest[-8:]
    rows = PATCH * GROUP
    groups = q_ref.shape[0]
    scale = jnp.asarray(HEAD ** (-0.5), BF16)

    @pl.when(pl.program_id(0) == 0)
    def _():
        key = lax.broadcasted_iota(jnp.int32, (rows, rows), 0)
        query = lax.broadcasted_iota(jnp.int32, (rows, rows), 1)
        same = key % GROUP == query % GROUP
        bias_ref[...] = jnp.where(same & (key // GROUP <= query // GROUP), 0.0, -1e30)
        own_ref[...] = same[:GROUP].astype(F32)

    low = lax.broadcasted_iota(jnp.int32, (rows, PAIR), 1) < HEAD

    def stack(value):
        zero = jnp.zeros_like(value)
        return jnp.concatenate([jnp.where(low, value, zero), jnp.where(low, zero, value)], axis=0)

    block = lambda ref, g: ref[g].reshape(rows, PAIR)
    for g in range(groups):
        s_ref[g] = dot(block(k_ref, g), stack(block(q_ref, g) * scale), NT)
        dp_ref[g] = dot(block(v_ref, g), stack(block(d_ref, g)), NT)
    for g in range(groups):
        for h in range(2):
            at = slice(h * rows, (h + 1) * rows)
            scores = (s_ref[g, :, at] + bias_ref[...]).reshape(PATCH, GROUP, rows)
            expo = jnp.exp(scores - jnp.max(scores, axis=0, keepdims=True))
            total = jnp.sum(expo, axis=0, keepdims=True)
            probs = expo * (own_ref[...] / total)
            d_probs = dp_ref[g, :, at].reshape(PATCH, GROUP, rows)
            d_scores = probs * (d_probs - jnp.sum(probs * d_probs, axis=0, keepdims=True))
            p_ref[g, :, at] = probs.astype(BF16).reshape(rows, rows)
            ds_ref[g, :, at] = d_scores.astype(BF16).reshape(rows, rows)
    for g in range(groups):
        k = block(k_ref, g)
        probs, d_scores = p_ref[g], ds_ref[g]
        context = dot(block(v_ref, g).T, probs).astype(BF16)
        at = slice(g * rows, (g + 1) * rows)
        context_ref[:HEAD, at] = context[:HEAD, :rows]
        context_ref[HEAD:, at] = context[HEAD:, rows:]
        d_query = dot(d_scores, k * scale, TN)
        d_query = jnp.where(low, d_query[:rows], d_query[rows:])
        d_key = dot(d_scores, stack(block(q_ref, g) * scale))
        d_value = dot(probs, stack(block(d_ref, g)))
        for n, grad in enumerate((d_query, d_key, d_value)):
            d_qkv_ref[n, g] = grad.astype(BF16).reshape(PATCH, GROUP, PAIR)


def attention(qkv, d_context, first, count, after=()):
    groups, _, _, width = d_context.shape
    pairs = width // PAIR
    tokens = groups * PATCH * GROUP
    spec = lambda part: pl.BlockSpec(
        (groups, PATCH, GROUP, PAIR), lambda n: (0, 0, 0, part * pairs + first + n)
    )
    return pl.pallas_call(
        attention_kernel,
        grid=(count,),
        in_specs=[spec(0), spec(1), spec(2), spec(0)]
        + [pl.BlockSpec(memory_space=pl.ANY)] * len(after),
        out_specs=[
            pl.BlockSpec((PAIR, tokens), lambda n: (n, 0)),
            pl.BlockSpec((3, groups, PATCH, GROUP, PAIR), lambda n: (0, 0, 0, 0, n)),
        ],
        out_shape=[
            jax.ShapeDtypeStruct((count * PAIR, tokens), BF16),
            jax.ShapeDtypeStruct((3, groups, PATCH, GROUP, count * PAIR), BF16),
        ],
        scratch_shapes=[
            pltpu.VMEM((PATCH * GROUP, PATCH * GROUP), F32),
            pltpu.VMEM((GROUP, PATCH * GROUP), F32),
            pltpu.VMEM((groups, PATCH * GROUP, 2 * PATCH * GROUP), F32),
            pltpu.VMEM((groups, PATCH * GROUP, 2 * PATCH * GROUP), F32),
            pltpu.VMEM((groups, PATCH * GROUP, 2 * PATCH * GROUP), BF16),
            pltpu.VMEM((groups, PATCH * GROUP, 2 * PATCH * GROUP), BF16),
        ],
        cost_estimate=cost(count * groups * 6 * 2 * 256 * 256 * 128, count * 1.6e6),
        compiler_params=pltpu.CompilerParams(vmem_limit_bytes=11 << 20),
        name="attention",
    )(qkv, qkv, qkv, d_context, *after)


def turn_rows(lhs, left_ref, orders, place, height):
    tokens = left_ref.shape[2]
    base = 0
    for ref in lhs:
        major = ref.ndim == 2
        cols = ref.shape[0] if major else ref.shape[-1]
        for m in range(0, cols, 256):
            if major:
                turned = ref[m : m + 256, :]
            else:
                turned = ref[..., m : m + 256].reshape(tokens, 256).T
            turned = turned.astype(left_ref.dtype)
            for n, (which, order) in enumerate(orders):
                for b in range(0, 256, height):
                    at = order[(base + m + b) // height] ^ place[which]
                    left_ref[n, pl.ds(pl.multiple_of(at * height, height), height), :] = turned[
                        b : b + height
                    ]
        base += cols


def grad_kernel(place, *refs, sources, orders, height, extra):
    lhs, rhs_ref, rest = refs[:sources], refs[sources], refs[sources + 1 :]
    if extra:
        marks_ref, gain_ref = rest[:2]
        marked_ref, column_ref = rest[-2:]
        rest = rest[:-2]
    left_ref, outs = rest[-1], rest[-1 - 2 * len(orders) : -1]
    _, rows, tokens = left_ref.shape
    step = pl.program_id(0)
    steps = pl.num_programs(0)

    @pl.when(step == 0)
    def _():
        turn_rows(lhs, left_ref, orders, place, height)

    def emit(n, rhs):
        keep_ref, send_ref = outs[2 * n], outs[2 * n + 1]
        for m in range(0, rows, 256):
            tile = dot(left_ref[n, m : m + 256, :].astype(BF16), rhs).astype(BF16)
            if m < rows // 2:
                keep_ref[m : m + 256, :] = tile
            else:
                send_ref[m - rows // 2 : m - rows // 2 + 256, :] = tile

    for n in range(len(orders)):
        blocks = steps // len(orders)
        last = 4 if extra else steps

        @pl.when((step >= n * blocks) & (step < jnp.minimum((n + 1) * blocks, last)))
        def _(n=n):
            emit(n, rhs_ref[...].reshape(tokens, rhs_ref.shape[-1]))

    if extra:
        keep_ref, send_ref = outs[-2:]
        half = rows // 2
        per = marks_ref.shape[-1] * height // rows

        @pl.when(step < 4)
        def _():
            marks = marks_ref[...].reshape(tokens, marks_ref.shape[-1])
            got = dot(marks, rhs_ref[...].reshape(tokens, rhs_ref.shape[-1]), TN)
            for p in range(rows // height):
                at = pl.multiple_of(p * height + step * per, per)
                marked_ref[pl.ds(at, per), :] = got[p * per : (p + 1) * per]

        @pl.when(step == 4)
        def _():
            keep_ref[...] = marked_ref[:half].astype(BF16)
            send_ref[...] = marked_ref[half:].astype(BF16)

        @pl.when(step == 5)
        def _():
            column = jnp.sum(gain_ref[...].T, axis=1, keepdims=True)
            which, order = orders[-1]
            for b in range(0, rows, height):
                at = pl.multiple_of((order[b // height] ^ place[which]) * height, height)
                column_ref[pl.ds(at, height), :] = jnp.broadcast_to(
                    column[b : b + height], (height, 256)
                )
            keep_ref[...] = column_ref[:half].astype(BF16)
            send_ref[...] = column_ref[half:].astype(BF16)


def grad_rows(place, kinds, lhs, rhs, devices, after=(), extra=()):
    rows = sum(a.shape[0] if a.ndim == 2 else a.shape[-1] for a in lhs)
    cols = rhs.shape[-1]
    stacked = rhs.ndim == 5
    planes = rhs.shape[0] if stacked else 1
    block = 256
    per = cols // block
    height = rows // devices
    steps = planes * per + (2 if extra else 0)
    whole = lambda a: pl.BlockSpec(
        a.shape, lambda n, s: (0,) * a.ndim, pipeline_mode=pl.Buffered(1)
    )
    if stacked:
        rhs_spec = pl.BlockSpec(
            (1,) + rhs.shape[1:4] + (block,), lambda n, s: (n // per, 0, 0, 0, n % per)
        )
    else:
        rhs_spec = pl.BlockSpec(
            rhs.shape[:-1] + (block,), lambda n, s: (0, 0, 0, jnp.minimum(n, per - 1))
        )
    tokens = rhs.shape[-2] * rhs.shape[-3] * rhs.shape[-4]
    each = steps // len(kinds)
    out = jax.ShapeDtypeStruct((rows // 2, each * block), BF16)
    out_specs = []
    for n in range(len(kinds)):
        spec = pl.BlockSpec(
            (rows // 2, block), lambda i, s, n=n: (0, jnp.clip(i - n * each, 0, each - 1))
        )
        out_specs += [spec, spec]
    scratch = [pltpu.VMEM((len(kinds), rows, tokens), F32 if height % 16 else BF16)]
    if extra:
        scratch += [pltpu.VMEM((rows, block), F32), pltpu.VMEM((rows, block), F32)]
    got = pl.pallas_call(
        functools.partial(
            grad_kernel,
            sources=len(lhs),
            orders=[(which, spots(stages, devices)) for which, stages in kinds],
            height=height,
            extra=bool(extra),
        ),
        grid_spec=pltpu.PrefetchScalarGridSpec(
            num_scalar_prefetch=1,
            grid=(steps,),
            in_specs=[whole(a) for a in lhs]
            + [rhs_spec]
            + [whole(a) for a in extra]
            + [pl.BlockSpec(memory_space=pl.ANY)] * len(after),
            out_specs=out_specs,
            scratch_shapes=scratch,
        ),
        out_shape=[out] * (2 * len(kinds)),
        cost_estimate=cost(2 * tokens * rows * steps * block, 2 * rows * steps * block + 4e6),
        compiler_params=pltpu.CompilerParams(vmem_limit_bytes=13 << 20),
        name="grad_rows",
    )(place, *lhs, rhs, *extra, *after)
    return [(got[n], got[n + 1]) for n in range(0, len(got), 2)]


def input_grad_kernel(*refs, chunks):
    d_refs, w_ref = refs[:chunks], refs[chunks]
    far, gain_ref = refs[chunks + 1 : chunks + 4], refs[chunks + 4]
    d_x_ref, grad_gain_ref, acc_ref, normed_ref, inv_ref, out_grad_ref, sems = refs[-7:]
    step = pl.program_id(0)
    near = (normed_ref, inv_ref, out_grad_ref)
    copies = [pltpu.make_async_copy(a, b, sems.at[n]) for n, (a, b) in enumerate(zip(far, near))]
    groups, _, _, width = normed_ref.shape
    rows = groups * PATCH * GROUP

    @pl.when(step == 0)
    def _():
        for copy in copies:
            copy.start()
        acc_ref[...] = jnp.zeros_like(acc_ref)

    d_qkv = [d_ref[...].reshape(rows, d_ref.shape[-1]) for d_ref in d_refs]
    d_qkv = jnp.concatenate(d_qkv, axis=1)
    for n in range(0, width, 256):
        acc_ref[:, n : n + 256] += dot(d_qkv, w_ref[n : n + 256, :], NT)

    @pl.when(step == pl.num_programs(0) - 1)
    def _():
        for copy in copies:
            copy.wait()
        grad_gain_ref[...] = jnp.zeros_like(grad_gain_ref)
        tiles = [slice(c, c + 128) for c in range(0, width, 128)]

        @pl.loop(0, groups)
        def _(g):
            at = [pl.multiple_of((g * PATCH + p) * GROUP, GROUP) for p in range(PATCH)]
            sums = [jnp.zeros((GROUP, 128), F32) for _ in range(PATCH)]
            for tile in tiles:
                total = jnp.zeros((GROUP, 128), F32)
                for p in range(PATCH):
                    part = acc_ref[pl.ds(at[p], GROUP), tile] * normed_ref[g, p, :, tile]
                    total = total + part
                    sums[p] = sums[p] + part * gain_ref[:, tile]
                grad_gain_ref[:, tile] += total[:8] + total[8:]
            for p in range(PATCH):
                mean = jnp.sum(sums[p], axis=1, keepdims=True) * (1.0 / width)
                inv = inv_ref[g, p]
                for tile in tiles:
                    d_normed = acc_ref[pl.ds(at[p], GROUP), tile] * gain_ref[:, tile]
                    d_x = inv * (d_normed - normed_ref[g, p, :, tile] * mean)
                    d_x = out_grad_ref[g, p, :, tile].astype(F32) + d_x
                    d_x_ref[g, p, :, tile] = d_x.astype(BF16)


def input_grad(d_qkvs, w_qkv, normed, inv, gain, out_grad, after=()):
    groups, _, _, width = normed.shape
    tokens = groups * PATCH * GROUP
    chunks = len(d_qkvs)
    d_specs = [
        pl.BlockSpec((1, groups, PATCH, GROUP, d.shape[-1]), lambda n: (n, 0, 0, 0, 0))
        for d in d_qkvs
    ]
    w_spec = pl.BlockSpec((width, width), lambda n: (0, n))
    whole = lambda a: pl.BlockSpec(
        a.shape, lambda n: (0,) * a.ndim, pipeline_mode=pl.Buffered(1)
    )
    return pl.pallas_call(
        functools.partial(input_grad_kernel, chunks=chunks),
        grid=(3,),
        in_specs=d_specs
        + [w_spec]
        + [pl.BlockSpec(memory_space=pl.ANY)] * 3
        + [whole(gain)]
        + [pl.BlockSpec(memory_space=pl.ANY)] * len(after),
        out_specs=[
            pl.BlockSpec(normed.shape, lambda n: (0, 0, 0, 0)),
            pl.BlockSpec((8, width), lambda n: (0, 0)),
        ],
        out_shape=[
            jax.ShapeDtypeStruct(normed.shape, BF16),
            jax.ShapeDtypeStruct((8, width), F32),
        ],
        scratch_shapes=[
            pltpu.VMEM((tokens, width), F32),
            pltpu.VMEM(normed.shape, F32),
            pltpu.VMEM(inv.shape, F32),
            pltpu.VMEM(out_grad.shape, BF16),
            pltpu.SemaphoreType.DMA((3,)),
        ],
        cost_estimate=cost(2 * tokens * width * 3 * width, 20e6),
        compiler_params=pltpu.CompilerParams(vmem_limit_bytes=20 << 20),
        name="input_grad",
    )(*map(in_hbm, d_qkvs), w_qkv, normed, inv, out_grad, gain, *after)


def back_kernel(place, d_x_ref, w_ref, *refs, count):
    outs, moved_ref = refs[-count - 1 : -1], refs[-1]
    groups, _, _, width = d_x_ref.shape
    rows = groups * PATCH * GROUP
    left = d_x_ref[...].reshape(rows, width)
    for n in range(0, width, 256):
        got = dot(left, w_ref[n : n + 256, :], NT).astype(BF16)
        got = got.reshape(groups, PATCH, GROUP, 256)
        for g in range(groups):
            for j in range(PATCH):
                moved_ref[j, g * GROUP : (g + 1) * GROUP, n : n + 256] = got[g, j]
    for k, out in enumerate(outs):
        for h in range(2):
            out[:, h * width : (h + 1) * width] = moved_ref[2 * (place[2] ^ k) + h]


def back(place, d_x, w_proj, tp, after=()):
    groups, _, _, width = d_x.shape
    half = groups * GROUP
    whole = lambda a: pl.BlockSpec(
        a.shape, lambda n, s: (0,) * a.ndim, pipeline_mode=pl.Buffered(1)
    )
    out = jax.ShapeDtypeStruct((half, 2 * width), BF16)
    return pl.pallas_call(
        functools.partial(back_kernel, count=tp),
        grid_spec=pltpu.PrefetchScalarGridSpec(
            num_scalar_prefetch=1,
            grid=(1,),
            in_specs=[whole(d_x), whole(w_proj)]
            + [pl.BlockSpec(memory_space=pl.ANY)] * len(after),
            out_specs=[whole(out)] * tp,
            scratch_shapes=[pltpu.VMEM((PATCH, half, width), BF16)],
        ),
        out_shape=[out] * tp,
        cost_estimate=cost(2 * PATCH * half * width * width, 6e6),
        compiler_params=pltpu.CompilerParams(vmem_limit_bytes=11 << 20),
        name="back",
    )(place, d_x, w_proj, *after)


def spots(stages, devices):
    order = scatter_order(stages)
    where = [0] * devices
    for p, q in enumerate(order):
        where[q] = p
    return where


def spot_of(value, stages, devices):
    where = spots(stages, devices)
    total = jnp.zeros_like(value)
    for bit in range(devices.bit_length() - 1):
        total = total + ((value >> bit) & 1) * where[1 << bit]
    return total


def on_device(mesh, glob_out, byte_ids, out_grad, embed, w_proj, norm_gain, w_qkv, w_out):
    vocab, width = embed.shape
    tp, devices = mesh.shape["tp"], mesh.size
    half = byte_ids.shape[0]
    groups = half // GROUP
    t = lax.axis_index("tp").astype(jnp.int32)
    me = lax.axis_index("seq").astype(jnp.int32) * tp + t
    tp_bits, seq_bits = bit_masks(mesh)
    core, wide = tp_bits[:1], tp_bits[1:]
    xy = [core, wide] + [[bit] for bit in seq_bits]
    yx = [core, seq_bits[:1], wide] + [[bit] for bit in seq_bits[1:]]
    yzx = [core] + [[bit] for bit in seq_bits] + [wide]
    place = jnp.stack([t >> 1, t & 1, t] + [spot_of(me, o, devices) for o in (xy, yx, yzx)])
    XY, YX, YZX = (3, xy), (4, yx), (5, yzx)

    arrived = {}
    for k in (2, 3, 1)[: tp - 1]:
        block = lax.dynamic_slice(glob_out, ((t ^ k) * half, 0), (half, glob_out.shape[1]))
        arrived[k] = exchange(block, k, devices)

    ids = byte_ids.reshape(groups, GROUP, PATCH).transpose(0, 2, 1)
    onehot = (ids[..., None] == jnp.arange(vocab, dtype=jnp.int32)).astype(BF16)
    grads = out_grad.reshape(groups, GROUP, PATCH, width).transpose(0, 2, 1, 3)
    d_context = lax.dot_general(
        grads, w_out, (((3,), (1,)), ((), ())), preferred_element_type=F32
    ).astype(BF16)
    gain = norm_gain.reshape(1, width)

    early = project(place, glob_out, arrived[1], onehot, embed, w_proj, gain, w_qkv, None)
    slices, normed, inv, act, qkv = project(
        place, arrived[2], arrived[3], onehot, embed, w_proj, gain, w_qkv, early
    )

    def hop(pairs, masks, mode="split"):
        arrived = []
        for (keep, send), mask in zip(pairs, masks):
            arrived.append((keep, exchange(send, mask, devices)))
        return combine(arrived, mode)

    flat = lambda pairs: [a for pair in pairs for a in pair]
    first, second = core[0], (wide[0], seq_bits[0])
    rest = seq_bits[1:]

    def finish(pairs, n=0):
        for bit in rest[n:-1]:
            pairs = hop(pairs, [bit])
            n += 1
        return hop(pairs, [rest[-1]], "last")[0]

    pairs = width // PAIR
    count = pairs // 2
    context_a, d_qkv_a = attention(qkv, d_context, 0, count)
    one = grad_rows(place, (XY, YX), [act], d_qkv_a, devices)
    context_b, d_qkv_b = attention(qkv, d_context, count, count, flat(one)[:1])
    one = hop(one, (first, first))
    two = grad_rows(place, (XY,), [act], d_qkv_b, devices)
    two = two + grad_rows(place, (YX,), [context_a, context_b], grads, devices, flat(two)[:1])
    one = hop(one, second)
    two = hop(two, (first, first))

    d_x, grad_gain = input_grad((d_qkv_a, d_qkv_b), w_qkv, normed, inv, gain, grads)
    one = hop(one, second[::-1], "merge")
    two = hop(two, second)

    height = vocab // devices
    spot = spot_of((ids // height) ^ me, yzx, devices) * height + ids % height
    marks = (spot[..., None] == jnp.arange(vocab, dtype=jnp.int32)).astype(BF16)
    fits = height % 8 == 0 and width == 4 * vocab
    extra = (marks, grad_gain) if fits else ()
    three = grad_rows(place, (XY, YZX), [slices], d_x, devices, (), extra)

    rows = back(place, d_x, w_proj, tp, flat(three)[:1])
    glob_grad = jnp.zeros((tp * half, 2 * width), BF16)
    for k in range(tp):
        piece = rows[0]
        if k:
            piece = exchange(rows[k], k, devices)
        glob_grad = lax.dynamic_update_slice(glob_grad, piece, ((t ^ k) * half, 0))

    two = hop(two, second[::-1], "merge")
    three = hop(three, (first, first))
    paths = list(zip([b[0] for b in xy[1:]], [b[0] for b in yzx[1:]]))
    for n, masks in enumerate(paths):
        last = n + 1 == len(paths)
        three = hop(three, masks, "last" if last else "split")
    one, two = finish(one), finish(two)

    each = width // devices
    if fits:
        cut = width - three[0].shape[1]
        grad_proj = jnp.concatenate([three[0], three[1][:, :cut]], axis=1)
        marked = three[1][:, cut : cut + 256].reshape(4, height, 256)
        grad_embed = marked.transpose(1, 0, 2).reshape(height, width)
        grad_gain = three[1][:, cut + 256]
    else:
        grad_proj = jnp.concatenate(three, axis=1)
        grad_embed = lax.dot_general(
            marks, d_x, (((0, 1, 2), (0, 1, 2)), ((), ())), preferred_element_type=F32
        ).astype(BF16)
        flips = [b[0] for b in yzx]
        grad_embed = split_scatter(grad_embed, flips, devices)
        blocks = jnp.sum(grad_gain, axis=0).reshape(devices, each)
        blocks = blocks[jnp.array(scatter_order(yzx), dtype=jnp.int32) ^ me]
        grad_gain = split_scatter(blocks, flips, devices).reshape(-1)

    span = count * PAIR
    grad_out = two[:, 3 * span :]
    grad_qkv = jnp.concatenate(
        [part[:, n * span : (n + 1) * span] for n in range(3) for part in (one, two)], axis=1
    )
    return (glob_grad, grad_embed, grad_proj, grad_gain, grad_qkv, grad_out)


def solution(mesh):
    def body(*args):
        return on_device(mesh, *args)

    return shard(body, mesh)


def shard(body, mesh):
    return jax.shard_map(
        body,
        mesh=mesh,
        in_specs=(
            P("seq", "tp"),
            P(AXES, None),
            P(AXES, None),
            P(),
            P(),
            P(),
            P(),
            P(),
        ),
        out_specs=(
            P("seq", "tp"),
            P(AXES, None),
            P(AXES, None),
            P(AXES),
            P(AXES, None),
            P(AXES, None),
        ),
        check_vma=False,
    )
```
